256 devices in a mesh: sec: 32 (over z, y), depth: 4 (over x), segment: 2 (over core).
Axes of the slice: x: 4, y: 4, z: 8, core: 2. Of those that a mesh axis runs over, the one named last changes fastest.
Arguments:
- fields: float32 [2, 9, 64, 64, 128], P('segment', None, 'sec', 'depth'), may hold values from -6 to 6
- block_ids: int32 [2, 64, 64, 128], P('segment', 'sec', 'depth'), may hold values from 0 to 15
- buoyancy: float32 [16], replicated, may hold values from 0.5 to 1
- lame_lambda: float32 [16], replicated, may hold values from 0.2 to 0.6
- lame_mu: float32 [16], replicated, may hold values from 0.1 to 0.3
- moments: float32 [6, 131072], P(None, ('sec', 'depth')), may hold values from -12 to 12
- moment_owner: int32 [131072, 1], P(('sec', 'depth')), may hold values from 0 to 31; in each aligned block of 1024 rows (0 to 1023, 1024 to 2047, ...) at most 64 rows name the same one
- moment_cells: int32 [131072], P(('sec', 'depth')), may hold values from 0 to 4095
- drm_rows: int32 [262144], P(('sec', 'depth')), may hold values from 0 to 4095
Outputs:
- final_fields: float32 [2, 9, 64, 64, 128], P('segment', None, 'sec', 'depth')
The draws below stay inside these ranges and needn't reach their ends.
Inputs may be any that keep to these rules, and one draw needn't show every extreme that they name: `moment_owner`: in the entries of one section and slab at most 64 name the same section, a bound that some block reaches of them.
All inputs are finite; a program needn't handle non-finite values.
Results may differ from the reference program's by a relative error of at most 0.00002.
Values sent between devices are 32-bit elements; how exact they have to be, the bound alone decides.
A program may use at most 64 MiB of HBM per device.

```python
import math
import jax
import jax.numpy as jnp
import numpy as np
from jax import lax

CX = 2
CZ = 16
CY = 128
STEPS = 4
NBLK = 16
ENT = 1024
R = 2048
CAP = 64
CELLS = 4096
NX = 64
NZ = 64
ENTS = 131072
ROWS = 262144
N_SEC = 32
N_DEPTH = 4


def with_ends(array, rng, low, top_value):
    spot = [jax.random.randint(jax.random.fold_in(rng, axis), (), 0, length) for axis, length in enumerate(array.shape)]
    longest = array.shape.index(max(array.shape))
    neighbour = spot[:longest] + [(spot[longest] + 1) % array.shape[longest]] + spot[longest + 1:]
    return array.at[tuple(spot)].set(low).at[tuple(neighbour)].set(top_value)


def levels(key, shape, shards, smallest, high):
    gain, own = 1.0, jax.random.fold_in(key, 6)
    for position, shards_of in shards:
        draws = jnp.exp(jax.random.uniform(jax.random.fold_in(own, position), (shards_of,), jnp.float32, smallest / len(shards), high / len(shards)))
        gain = gain * jnp.repeat(draws, shape[position] // shards_of).reshape([-1 if axis == position else 1 for axis in range(len(shape))])
    return gain


def shared_out(rng, own, number, rows, number_of, top, limit, slope):
    sequence = jax.random.permutation(rng, number_of)
    crowded, usual = load_shares(number_of, rows * top, limit, slope, True), load_shares(number_of, rows * top, limit, slope, False)
    places = jnp.arange(number_of)

    def named(tallies, offset_by):
        used = int((tallies > 0).sum())
        fixed = max(1, used // 4)
        passed = fixed + (places - fixed + offset_by * (used - fixed)) % max(1, number_of - fixed)
        return jnp.zeros((number_of,), jnp.int32).at[sequence[jnp.where(places < fixed, places, passed)]].set(jnp.asarray(tallies, jnp.int32))

    tallies = jnp.where(number % 4 == 0, named(crowded, number // 4), named(usual, number - number // 4 - 1))
    mixed = jax.random.permutation(jax.random.fold_in(own, 3), number_of)
    donor, sink = mixed[0:number_of // 2 * 2:2], mixed[1:number_of // 2 * 2:2]
    room = jnp.minimum(tallies[donor] - 1, limit - tallies[sink]) // 2
    room = jnp.where((donor == sequence[0]) | (sink == sequence[0]) | (tallies[sink] == 0), 0, jnp.maximum(room, 0))
    passed = jax.random.randint(jax.random.fold_in(own, 4), (number_of // 2,), 0, 1 << 20) % (room + 1)
    tallies = tallies.at[donor].add(-passed).at[sink].add(passed)
    members = jnp.searchsorted(jnp.cumsum(tallies), jnp.arange(rows * top), side="right").astype(jnp.int32)
    listing = members.reshape(top, rows).T
    listing = listing[jax.random.permutation(jax.random.fold_in(own, 1), rows)]
    offset_by = jax.random.randint(jax.random.fold_in(own, 2), (rows, 1), 0, top)
    return jnp.take_along_axis(listing, (jnp.arange(top)[None, :] + offset_by) % top, axis=1)


def load_shares(count, total, most, slope, full):
    weights = [(1 << 20) // math.isqrt(standing ** slope) + 1 for standing in range(1, count + 1)]
    largest = most if full else min(most, max(-(-total // count), total * weights[0] // sum(weights)))
    least = 1 if total - largest >= count - 1 else 0
    given, surplus = [largest] + [least] * (count - 1), total - largest - least * (count - 1)
    while surplus > 0:
        candidates = [i for i in range(1, count) if given[i] < largest] or [i for i in range(1, count) if given[i] < most]
        mass, left = sum([weights[i] for i in candidates]), surplus
        for i in candidates:
            extra = min(most - given[i], max(1, left * weights[i] // mass), surplus)
            given[i] = given[i] + extra
            surplus = surplus - extra
    return np.array(given)


def noise(rng, dims, scale, limit, cuts=(), kind=jnp.bfloat16):
    values = jax.random.normal(rng, dims, jnp.float32) * scale
    if len(cuts) > 0:
        values = levels(rng, dims, cuts, -0.22, 0.18) * values
    return jnp.clip(values, min=-limit, max=limit).astype(kind)


def setup_inputs(seed: int = 0) -> dict:
    key_list = jax.random.split(jax.random.key(seed), 10)
    fields = noise(key_list[0], (2, 9, NX, NZ, CY), 1.0, 6.0, ((0, 2), (2, 32), (3, 4)), jnp.float32)
    block_ids = with_ends(jax.random.randint(key_list[1], (2, NX, NZ, CY), 0, NBLK), jax.random.fold_in(key_list[1], 1), 0, NBLK - 1).astype(jnp.int32)
    buoyancy = jnp.clip(jnp.exp(jax.random.uniform(key_list[2], (NBLK,), jnp.float32, math.log(0.5), math.log(1.0))), 0.5, 1.0)
    lame_lambda = jnp.clip(jax.random.uniform(key_list[3], (NBLK,), jnp.float32, 0.2, 0.6), 0.2, 0.6)
    lame_mu = jnp.clip(jax.random.uniform(key_list[4], (NBLK,), jnp.float32, 0.1, 0.3), 0.1, 0.3)
    moments = noise(key_list[5], (6, ENTS), 2.0, 12.0, ((1, 128),), jnp.float32)
    moment_owner_keys = jax.random.split(jax.random.fold_in(key_list[6], 1), ENTS // ENT)
    moment_owner_turns = jax.random.permutation(jax.random.fold_in(key_list[6], 3), ENTS // ENT)
    moment_owner = jax.vmap(lambda own, number: shared_out(jax.random.fold_in(key_list[6], 2), own, number, ENT, N_SEC, 1, CAP, 2))(moment_owner_keys, moment_owner_turns).reshape((ENTS, 1))
    moment_cells = with_ends(jax.random.randint(key_list[7], (ENTS,), 0, CELLS), jax.random.fold_in(key_list[7], 1), 0, CELLS - 1).astype(jnp.int32)
    drm_rows = with_ends(jax.random.randint(key_list[8], (ROWS,), 0, CELLS), jax.random.fold_in(key_list[8], 1), 0, CELLS - 1).astype(jnp.int32)
    return {"fields": fields, "block_ids": block_ids, "buoyancy": buoyancy, "lame_lambda": lame_lambda, "lame_mu": lame_mu, "moments": moments, "moment_owner": moment_owner, "moment_cells": moment_cells, "drm_rows": drm_rows}


HALF_STEP = 0.5


def lookup(block_ids, table):
    result = jnp.zeros(block_ids.shape, jnp.float32)
    for entry in range(table.shape[0]):
        result = result + jnp.where(block_ids == entry, table[entry], jnp.float32(0.0))
    return result


def back_diff(field, axis):
    count = field.shape[axis]
    first = jnp.zeros_like(lax.slice_in_dim(field, 0, 1, axis=axis))
    before = jnp.concatenate([first, lax.slice_in_dim(field, 0, count - 1, axis=axis)], axis)
    return field - before


def fore_diff(field, axis):
    count = field.shape[axis]
    last = jnp.zeros_like(lax.slice_in_dim(field, 0, 1, axis=axis))
    after = jnp.concatenate([lax.slice_in_dim(field, 1, count, axis=axis), last], axis)
    return after - field


def reference(fields, block_ids, buoyancy, lame_lambda, lame_mu, moments, moment_owner, moment_cells, drm_rows):
    buoy = lookup(block_ids, buoyancy)
    lam = lookup(block_ids, lame_lambda)
    shear = lookup(block_ids, lame_mu)
    entries = jnp.arange(ENTS, dtype=jnp.int32)
    slab = (entries // ENT) % N_DEPTH
    gx = moment_owner[:, 0] * CX + moment_cells // (CZ * CY)
    gz = slab * CZ + (moment_cells // CY) % CZ
    gy = moment_cells % CY
    target = ((gx * NZ + gz) * CY + gy).astype(jnp.int32)
    stress = fields[0, 3:].reshape(6, -1).at[:, target].add(moments)
    state = fields.at[0, 3:].set(stress.reshape(6, NX, NZ, CY))
    rows = jnp.arange(ROWS, dtype=jnp.int32)
    owner_dev = rows // R
    rsec = owner_dev // N_DEPTH
    rslab = owner_dev % N_DEPTH
    rx = rsec * CX + drm_rows // (CZ * CY)
    rz = rslab * CZ + (drm_rows // CY) % CZ
    ry = drm_rows % CY
    boundary = ((rx * NZ + rz) * CY + ry).astype(jnp.int32)
    for step in range(STEPS):
        vx, vy, vz = state[:, 0], state[:, 1], state[:, 2]
        sxx, syy, szz, syz, sxz, sxy = (state[:, k] for k in range(3, 9))
        nvx = vx + HALF_STEP * buoy * (back_diff(sxx, 1) + back_diff(sxy, 3) + back_diff(sxz, 2))
        nvy = vy + HALF_STEP * buoy * (back_diff(sxy, 1) + back_diff(syy, 3) + back_diff(syz, 2))
        nvz = vz + HALF_STEP * buoy * (back_diff(sxz, 1) + back_diff(syz, 3) + back_diff(szz, 2))
        newv = jnp.stack([nvx, nvy, nvz], axis=1)
        oldv = state[:, :3]
        increment = (newv[0] - oldv[0]).reshape(3, -1)[:, boundary]
        basin = newv[1].reshape(3, -1).at[:, boundary].add(increment)
        newv = jnp.stack([newv[0], basin.reshape(3, NX, NZ, CY)], axis=0)
        vx, vy, vz = newv[:, 0], newv[:, 1], newv[:, 2]
        exx = fore_diff(vx, 1)
        eyy = fore_diff(vy, 3)
        ezz = fore_diff(vz, 2)
        trace = exx + eyy + ezz
        sxx = sxx + HALF_STEP * (lam * trace + 2.0 * shear * exx)
        syy = syy + HALF_STEP * (lam * trace + 2.0 * shear * eyy)
        szz = szz + HALF_STEP * (lam * trace + 2.0 * shear * ezz)
        syz = syz + HALF_STEP * shear * (fore_diff(vy, 2) + fore_diff(vz, 3))
        sxz = sxz + HALF_STEP * shear * (fore_diff(vx, 2) + fore_diff(vz, 1))
        sxy = sxy + HALF_STEP * shear * (fore_diff(vx, 3) + fore_diff(vy, 1))
        state = jnp.stack([vx, vy, vz, sxx, syy, szz, syz, sxz, sxy], axis=1)
    return state
```

```python
import functools

import jax
import jax.numpy as jnp
from jax import lax
from jax.experimental import pallas as pl
from jax.experimental.pallas import tpu as pltpu
from jax.sharding import PartitionSpec as P

MESH = pl.DeviceIdType.MESH
CX, CZ, CY = 2, 16, 128
ENT, ROWS, CAP, BUCKETS = 1024, 2048, 64, 32
PX, RZ = CX + 4, 24
X0, Z0 = 2, 4
OWN_X = slice(X0, X0 + CX)
OWN_Z = slice(Z0, Z0 + CZ)
NEAR = tuple((dx, dz) for dx in (-1, 0, 1) for dz in (-1, 0, 1) if (dx, dz) != (0, 0))
NT = (((1,), (1,)), ((), ()))
BF16, F32, I32 = jnp.bfloat16, jnp.float32, jnp.int32


def split(value):
    high = value.astype(BF16).astype(F32)
    return high, value - high


def source_z(dz):
    return {-1: (0, 2), 0: (0, CZ), 1: (CZ - 2, 2)}[dz]


def target_z(dz):
    return {-1: Z0 + CZ, 0: Z0, 1: Z0 - 2}[dz]


def target_x(dx):
    return X0 - CX * dx


def in_range(sec, depth, n_sec, n_depth):
    ok_sec = jnp.logical_and(sec >= 0, sec < n_sec)
    ok_depth = jnp.logical_and(depth >= 0, depth < n_depth)
    return jnp.logical_and(ok_sec, ok_depth)


def fill_buckets(owner, cells, mom, bucket, lhs, rhs):
    owners = [owner[t:t + 1, :] for t in range(8)]
    row32 = lax.broadcasted_iota(I32, (BUCKETS, 128), 0)
    hot = [jnp.where(row32 == o, 1.0, 0.0) for o in owners]
    before = jnp.where(
        lax.broadcasted_iota(I32, (128, 256), 0) < lax.broadcasted_iota(I32, (128, 256), 1), 1.0, 0.0
    ).astype(BF16)
    counts = jnp.dot(jnp.concatenate(hot, 0).astype(BF16), before, preferred_element_type=F32)
    running = jnp.zeros((BUCKETS, 128), F32)
    row16 = lax.broadcasted_iota(I32, (16, 128), 0)
    row256 = lax.broadcasted_iota(I32, (256, 128), 0)
    for t in range(8):
        part = counts[t * BUCKETS:(t + 1) * BUCKETS]
        rank = jnp.sum(hot[t] * (part[:, :128] + running), axis=0, keepdims=True).astype(I32)
        running = running + part[:, 128:]
        cols = slice(t * 128, (t + 1) * 128)
        slot = (owners[t] & 1) * 128 + rank
        mine = row16 == (owners[t] >> 1)
        cell = cells[t:t + 1, :].astype(F32)
        for h in range(2):
            at = slice((2 * t + h) * 128, (2 * t + h + 1) * 128)
            rhs[:, at] = jnp.where(row256 == slot + h * CAP, 1.0, 0.0).astype(BF16)
            for j in range(4):
                value = mom[2 * j + h:2 * j + h + 1, cols] if j < 3 else cell
                high, low = split(value)
                lhs[j * 16:(j + 1) * 16, at] = jnp.where(mine, high, 0.0).astype(BF16)
                lhs[64 + j * 16:64 + (j + 1) * 16, at] = jnp.where(mine, low, 0.0).astype(BF16)
    sums = lax.dot_general(lhs[0:128, :], rhs[...], NT, preferred_element_type=F32)
    sums = sums[0:64] + sums[64:128]
    for j in range(4):
        for x in range(2):
            bucket[x * 16:(x + 1) * 16, j, :] = sums[j * 16:(j + 1) * 16, x * 128:(x + 1) * 128]


def place(cell):
    return (cell >> 7) & 15, ((cell >> 11) << 7) | (cell & 127)


def add_buckets(arrived, state, leaving, lhs, rhs):
    low_half = lax.broadcasted_iota(I32, (16, 128), 1) < CAP
    values, cell = [], None
    for j in range(4):
        rows = arrived[:, j, :]
        a, b = rows[0:16], rows[16:32]
        even = jnp.where(low_half, a, pltpu.roll(b, CAP, 1))
        if j < 3:
            values.append(even)
            values.append(jnp.where(low_half, pltpu.roll(a, CAP, 1), b))
        else:
            cell = even.astype(I32)
    z, lane = place(cell)
    parts = [split(value) for value in values]
    row16 = lax.broadcasted_iota(I32, (16, 128), 0)
    row256 = lax.broadcasted_iota(I32, (256, 128), 0)
    for t in range(16):
        at = slice(t * 128, (t + 1) * 128)
        mine = row16 == z[t:t + 1]
        rhs[:, at] = jnp.where(row256 == lane[t:t + 1], 1.0, 0.0).astype(BF16)
        for k, (high, low) in enumerate(parts):
            lhs[k * 16:(k + 1) * 16, at] = jnp.where(mine, high[t:t + 1], 0.0).astype(BF16)
            lhs[96 + k * 16:96 + (k + 1) * 16, at] = jnp.where(mine, low[t:t + 1], 0.0).astype(BF16)
    sums = lax.dot_general(lhs[...], rhs[...], NT, preferred_element_type=F32)
    sums = sums[0:96] + sums[96:192]
    for k in range(6):
        for x in range(CX):
            total = state[3 + k, X0 + x, OWN_Z, :] + sums[k * 16:(k + 1) * 16, x * 128:(x + 1) * 128]
            state[3 + k, X0 + x, OWN_Z, :] = total
            leaving[3 + k, x] = total


def count_rows(rows, counts, lhs, rhs):
    z, lane = place(rows[...])
    row16 = lax.broadcasted_iota(I32, (16, 128), 0)
    row256 = lax.broadcasted_iota(I32, (256, 128), 0)
    for t in range(16):
        at = slice(t * 128, (t + 1) * 128)
        lhs[0:16, at] = jnp.where(row16 == z[t:t + 1], 1.0, 0.0).astype(BF16)
        rhs[:, at] = jnp.where(row256 == lane[t:t + 1], 1.0, 0.0).astype(BF16)
    sums = lax.dot_general(lhs[0:16, :], rhs[...], NT, preferred_element_type=F32)
    for x in range(CX):
        counts[X0 + x, OWN_Z, :] = sums[:, x * 128:(x + 1) * 128]


def look_up(ids, tables, coefs):
    for p in range(PX):
        block = ids[p]
        values = [jnp.zeros((RZ, CY), F32) for _ in tables]
        for entry in range(16):
            here = block == entry
            values = [jnp.where(here, table[entry], v) for table, v in zip(tables, values)]
        for k, v in enumerate(values):
            coefs[k, p] = 0.5 * v


def y_before(f, first):
    return jnp.where(first, 0.0, pltpu.roll(f, 1, 1))


def y_after(f, last):
    return jnp.where(last, 0.0, pltpu.roll(f, CY - 1, 1))


def z_before(f):
    return pltpu.roll(f, 1, 0)


def z_after(f):
    return pltpu.roll(f, RZ - 1, 0)


def increments(state, coefs, p):
    first = lax.broadcasted_iota(I32, (RZ, CY), 1) == 0
    b = coefs[0, p]
    sxx, syy, szz, syz, sxz, sxy = (state[k, p] for k in range(3, 9))
    bxx, bxz, bxy = (state[k, p - 1] for k in (3, 7, 8))
    ix = b * ((sxx - bxx) + (sxy - y_before(sxy, first)) + (sxz - z_before(sxz)))
    iy = b * ((sxy - bxy) + (syy - y_before(syy, first)) + (syz - z_before(syz)))
    iz = b * ((sxz - bxz) + (syz - y_before(syz, first)) + (szz - z_before(szz)))
    return ix, iy, iz


def stress(state, coefs, p):
    last = lax.broadcasted_iota(I32, (RZ, CY), 1) == CY - 1
    lam, mu = coefs[1, p], coefs[2, p]
    vx, vy, vz = (state[k, p] for k in range(3))
    ax, ay, az = (state[k, p + 1] for k in range(3))
    exx = ax - vx
    eyy = y_after(vy, last) - vy
    ezz = z_after(vz) - vz
    bulk = lam * (exx + eyy + ezz)
    mu2 = mu + mu
    state[3, p] += bulk + mu2 * exx
    state[4, p] += bulk + mu2 * eyy
    state[5, p] += bulk + mu2 * ezz
    state[6, p] += mu * ((z_after(vy) - vy) + (y_after(vz, last) - vz))
    state[7, p] += mu * ((z_after(vx) - vx) + (az - vz))
    state[8, p] += mu * ((y_after(vx, last) - vx) + (ay - vy))


def kernel(
    n_sec, n_depth, fields, block_ids, buoyancy, lame_lambda, lame_mu, moments, owners, cells, rows, out,
    state_a, state_b, leave_a, leave_b, ids, counts, coefs, incs, owner_v, cells_v, rows_v, mom_v, bucket, arrived, lhs, rhs,
    local_sem, raw_send, raw_recv, ids_send, ids_recv, count_send, count_recv, all_send, all_recv,
    first_send, first_recv, second_send, second_recv, inc_send, inc_recv,
):
    sec, depth, seg = lax.axis_index("sec"), lax.axis_index("depth"), lax.axis_index("segment")
    regional, basin = seg == 0, seg == 1

    state_a[...] = jnp.zeros_like(state_a)
    state_b[...] = jnp.zeros_like(state_b)
    ids[...] = jnp.full_like(ids, -1)
    counts[...] = jnp.zeros_like(counts)
    if n_sec < BUCKETS:
        arrived[...] = jnp.zeros_like(arrived)

    barrier = pltpu.get_barrier_semaphore()
    pl.semaphore_signal(barrier, inc=1, device_id=(sec, depth, 1 - seg), device_id_type=MESH)
    expected = jnp.int32(1)
    for dx, dz in NEAR:
        near = in_range(sec + dx, depth + dz, n_sec, n_depth)
        if dz == 0:
            near = jnp.logical_and(near, basin)
        expected = expected + near.astype(I32)

        @pl.when(near)
        def _():
            pl.semaphore_signal(barrier, inc=1, device_id=(sec + dx, depth + dz, seg), device_id_type=MESH)

    @pl.when(regional)
    def _():
        @pl.loop(1, n_sec)
        def _(j):
            pl.semaphore_signal(barrier, inc=1, device_id=(lax.rem(sec + j, n_sec), depth, seg), device_id_type=MESH)

    def load(k, src, dst):
        return pltpu.make_async_copy(src, dst, local_sem.at[k])

    own_state = load(0, fields.at[0], state_a.at[:, OWN_X, OWN_Z])
    own_ids = load(1, block_ids.at[0], ids.at[OWN_X, OWN_Z])
    own_state.start()
    own_ids.start()
    sorting = [load(2, owners, owner_v), load(3, cells, cells_v), load(4, moments, mom_v)]
    counting = load(2, rows, rows_v)

    @pl.when(regional)
    def _():
        for copy in sorting:
            copy.start()
        for copy in sorting:
            copy.wait()
        fill_buckets(owner_v, cells_v, mom_v, bucket, lhs, rhs)
        arrived[sec] = bucket[(sec % 2) * 16 + sec // 2]

    @pl.when(basin)
    def _():
        counting.start()
        counting.wait()
        count_rows(rows_v, counts, lhs, rhs)

    pl.semaphore_wait(barrier, expected + jnp.where(regional, n_sec - 1, 0))

    def passed(j):
        to = lax.rem(sec + j, n_sec)
        return pltpu.make_async_remote_copy(
            src_ref=bucket.at[(to % 2) * 16 + to // 2], dst_ref=arrived.at[sec],
            send_sem=all_send.at[j], recv_sem=all_recv.at[j], device_id=(to, depth, seg), device_id_type=MESH,
        )

    @pl.when(regional)
    def _():
        @pl.loop(0, n_sec - 1)
        def _(t):
            passed(1 + lax.rem(t + n_sec // 2 - 1, n_sec - 1)).start()

    class Exchange:
        def __init__(self, cond, send, recv, source, target):
            self.copies = []
            for q, (dx, dz) in enumerate(NEAR):
                start, size = source_z(dz)
                to = (sec + dx, depth + dz, seg)
                copy = pltpu.make_async_remote_copy(
                    src_ref=source(start, size),
                    dst_ref=target(slice(target_x(dx), target_x(dx) + CX), slice(target_z(dz), target_z(dz) + size)),
                    send_sem=send.at[q], recv_sem=recv.at[q], device_id=to, device_id_type=MESH,
                )
                sends = in_range(sec + dx, depth + dz, n_sec, n_depth)
                gets = in_range(sec - dx, depth - dz, n_sec, n_depth)
                if cond is not None:
                    sends, gets = jnp.logical_and(sends, cond), jnp.logical_and(gets, cond)
                self.copies.append((copy, sends, gets))

        def start(self):
            for copy, sends, _ in self.copies:
                pl.when(sends)(copy.start)

        def wait_recv(self):
            for copy, _, gets in self.copies:
                pl.when(gets)(copy.wait_recv)

        def wait_send(self):
            for copy, sends, _ in self.copies:
                pl.when(sends)(copy.wait_send)

    def own_z(start, size):
        return slice(Z0 + start, Z0 + start + size)

    def cut(start, size):
        return slice(start, start + size)

    raw_all = Exchange(
        basin, raw_send, raw_recv, lambda s, n: fields.at[0, :, :, s:s + n], lambda x, z: state_a.at[:, x, z]
    )
    raw_v = Exchange(
        regional, raw_send, raw_recv, lambda s, n: fields.at[0, 0:3, :, s:s + n], lambda x, z: state_a.at[0:3, x, z]
    )
    raw_ids = Exchange(
        None, ids_send, ids_recv, lambda s, n: block_ids.at[0, :, s:s + n], lambda x, z: ids.at[x, z]
    )
    raw_counts = Exchange(
        basin, count_send, count_recv, lambda s, n: counts.at[OWN_X, own_z(s, n)], lambda x, z: counts.at[x, z]
    )
    first = Exchange(
        regional, first_send, first_recv,
        lambda s, n: leave_a.at[3:9, :, cut(s, n)], lambda x, z: state_a.at[3:9, x, z],
    )
    second = Exchange(
        None, second_send, second_recv,
        lambda s, n: leave_b.at[:, :, cut(s, n)], lambda x, z: state_b.at[:, x, z],
    )
    raw_ids.start()
    raw_v.start()
    raw_all.start()
    raw_counts.start()

    own_ids.wait()
    raw_ids.wait_recv()
    look_up(ids, (buoyancy, lame_lambda, lame_mu), coefs)
    own_state.wait()

    @pl.when(regional)
    def _():
        @pl.loop(1, n_sec)
        def _(j):
            come = lax.rem(sec + n_sec - j, n_sec)
            pltpu.make_async_remote_copy(
                src_ref=bucket.at[0], dst_ref=arrived.at[come], send_sem=all_send.at[j], recv_sem=all_recv.at[j],
                device_id=(come, depth, seg), device_id_type=MESH,
            ).wait_recv()

        add_buckets(arrived, state_a, leave_a, lhs, rhs)

    first.start()
    raw_v.wait_recv()
    raw_all.wait_recv()
    raw_counts.wait_recv()
    first.wait_recv()

    def coupled(step, p):
        return pltpu.make_async_remote_copy(
            src_ref=incs.at[step, :, p], dst_ref=incs.at[step, :, p], send_sem=inc_send.at[step, p],
            recv_sem=inc_recv.at[step, p], device_id=(sec, depth, 1), device_id_type=MESH,
        )

    def advance(state, step, planes):
        @pl.when(regional)
        def _():
            for p in planes:
                for k, inc in enumerate(increments(state, coefs, p)):
                    incs[step, k, p] = inc
                    state[k, p] += inc
                coupled(step, p).start()

        @pl.when(basin)
        def _():
            for p in planes:
                mine = increments(state, coefs, p)
                coupled(step, p).wait_recv()
                count = counts[p]
                for k, inc in enumerate(mine):
                    state[k, p] += inc + count * incs[step, k, p]

        for p in planes[:-1]:
            stress(state, coefs, p)

    wide, narrow = range(X0 - 1, X0 + CX + 2), range(X0, X0 + CX + 1)
    advance(state_a, 0, wide)
    advance(state_a, 1, narrow)
    half_way = state_a[:, OWN_X, OWN_Z]
    leave_b[...] = half_way
    state_b[:, OWN_X, OWN_Z] = half_way
    second.start()
    second.wait_recv()
    advance(state_b, 2, wide)
    advance(state_b, 3, narrow)

    result = load(5, state_b.at[:, OWN_X, OWN_Z], out.at[0])
    result.start()

    raw_ids.wait_send()
    raw_v.wait_send()
    raw_all.wait_send()
    raw_counts.wait_send()
    first.wait_send()
    second.wait_send()

    @pl.when(regional)
    def _():
        @pl.loop(1, n_sec)
        def _(j):
            passed(j).wait_send()

        for step in range(4):
            for p in (wide, narrow)[step % 2]:
                coupled(step, p).wait_send()

    result.wait()


def on_device(
    n_sec, n_depth, fields, block_ids, buoyancy, lame_lambda, lame_mu, moments, moment_owner, moment_cells, drm_rows
):
    owners = moment_owner.reshape(ENT // 128, 128)
    cells = moment_cells.reshape(ENT // 128, 128)
    rows = drm_rows.reshape(ROWS // 128, 128)
    hbm = pl.BlockSpec(memory_space=pl.ANY)
    smem = pl.BlockSpec(memory_space=pltpu.SMEM)
    dma = pltpu.SemaphoreType.DMA
    near = [dma((len(NEAR),))] * 2
    block = (9, PX, RZ, CY)
    return pl.pallas_call(
        functools.partial(kernel, n_sec, n_depth),
        out_shape=jax.ShapeDtypeStruct(fields.shape, F32),
        in_specs=[hbm, hbm, smem, smem, smem, hbm, hbm, hbm, hbm],
        out_specs=hbm,
        scratch_shapes=[
            pltpu.VMEM(block, F32),
            pltpu.VMEM(block, F32),
            pltpu.VMEM((9, CX, CZ, CY), F32),
            pltpu.VMEM((9, CX, CZ, CY), F32),
            pltpu.VMEM(block[1:], I32),
            pltpu.VMEM(block[1:], F32),
            pltpu.VMEM((3,) + block[1:], F32),
            pltpu.VMEM((4, 3) + block[1:], F32),
            pltpu.VMEM((ENT // 128, 128), I32),
            pltpu.VMEM((ENT // 128, 128), I32),
            pltpu.VMEM((ROWS // 128, 128), I32),
            pltpu.VMEM((6, ENT), F32),
            pltpu.VMEM((BUCKETS, 4, 128), F32),
            pltpu.VMEM((BUCKETS, 4, 128), F32),
            pltpu.VMEM((192, 2048), BF16),
            pltpu.VMEM((256, 2048), BF16),
            dma((6,)),
            *near, *near, *near,
            dma((BUCKETS,)), dma((BUCKETS,)),
            *near, *near,
            dma((4, PX)), dma((4, PX)),
        ],
        compiler_params=pltpu.CompilerParams(collective_id=0, has_side_effects=True),
    )(fields, block_ids, buoyancy, lame_lambda, lame_mu, moments, owners, cells, rows)


def solution(mesh):
    in_specs = (
        P("segment", None, "sec", "depth", None),
        P("segment", "sec", "depth", None),
        P(),
        P(),
        P(),
        P(None, ("sec", "depth")),
        P(("sec", "depth"), None),
        P(("sec", "depth")),
        P(("sec", "depth")),
    )
    return jax.shard_map(
        functools.partial(on_device, mesh.shape["sec"], mesh.shape["depth"]),
        mesh=mesh, in_specs=in_specs, out_specs=P("segment", None, "sec", "depth", None), check_vma=False,
    )
```

```python
import functools

import jax
import jax.numpy as jnp
from jax import lax
from jax.experimental import pallas as pl
from jax.experimental.pallas import tpu as pltpu
from jax.sharding import PartitionSpec as P

MESH = pl.DeviceIdType.MESH
CX, CZ, CY = 2, 16, 128
ENT, ROWS, CAP, BUCKETS = 1024, 2048, 64, 32
HZ, RIM = CZ // 2, 4
PX, RZ, GZ = CX + 4, HZ + 2 * RIM, CZ + 2 * RIM
X0 = 2
OWN_X, OWN_Z = slice(X0, X0 + CX), slice(RIM, RIM + HZ)
NEAR = tuple((dx, dz) for dx in (-1, 0, 1) for dz in (-1, 0, 1) if (dx, dz) != (0, 0))
NT = (((1,), (1,)), ((), ()))
BF16, F32, I32 = jnp.bfloat16, jnp.float32, jnp.int32


def split(value):
    high = value.astype(BF16).astype(F32)
    return high, value - high


def rows_at(start, size):
    return slice(start, start + size)


def beside(dx):
    return rows_at(X0 - CX * dx, CX)


def in_range(sec, depth, n_sec, n_depth):
    ok_sec = jnp.logical_and(sec >= 0, sec < n_sec)
    ok_depth = jnp.logical_and(depth >= 0, depth < n_depth)
    return jnp.logical_and(ok_sec, ok_depth)


def fill_buckets(owner, cells, mom, bucket, lhs, rhs):
    owners = [owner[t:t + 1, :] for t in range(8)]
    row32 = lax.broadcasted_iota(I32, (BUCKETS, 128), 0)
    hot = [jnp.where(row32 == o, 1.0, 0.0) for o in owners]
    before = jnp.where(
        lax.broadcasted_iota(I32, (128, 256), 0) < lax.broadcasted_iota(I32, (128, 256), 1), 1.0, 0.0
    ).astype(BF16)
    counts = jnp.dot(jnp.concatenate(hot, 0).astype(BF16), before, preferred_element_type=F32)
    running = jnp.zeros((BUCKETS, 128), F32)
    row16 = lax.broadcasted_iota(I32, (16, 128), 0)
    row256 = lax.broadcasted_iota(I32, (256, 128), 0)
    for t in range(8):
        part = counts[t * BUCKETS:(t + 1) * BUCKETS]
        rank = jnp.sum(hot[t] * (part[:, :128] + running), axis=0, keepdims=True).astype(I32)
        running = running + part[:, 128:]
        cols = slice(t * 128, (t + 1) * 128)
        slot = (owners[t] & 1) * 128 + rank
        mine = row16 == (owners[t] >> 1)
        cell = cells[t:t + 1, :].astype(F32)
        for h in range(2):
            at = slice((2 * t + h) * 128, (2 * t + h + 1) * 128)
            rhs[:, at] = jnp.where(row256 == slot + h * CAP, 1.0, 0.0).astype(BF16)
            for j in range(4):
                value = mom[2 * j + h:2 * j + h + 1, cols] if j < 3 else cell
                high, low = split(value)
                lhs[j * 16:(j + 1) * 16, at] = jnp.where(mine, high, 0.0).astype(BF16)
                lhs[64 + j * 16:64 + (j + 1) * 16, at] = jnp.where(mine, low, 0.0).astype(BF16)
    sums = lax.dot_general(lhs[0:128, :], rhs[...], NT, preferred_element_type=F32)
    sums = sums[0:64] + sums[64:128]
    for j in range(4):
        for x in range(2):
            bucket[x * 16:(x + 1) * 16, j, :] = sums[j * 16:(j + 1) * 16, x * 128:(x + 1) * 128]


def place(cell):
    return (cell >> 7) & 15, ((cell >> 11) << 7) | (cell & 127)


def add_buckets(arrived, raw, leaving, lhs, rhs):
    low_half = lax.broadcasted_iota(I32, (16, 128), 1) < CAP
    values, cell = [], None
    for j in range(4):
        rows = arrived[:, j, :]
        a, b = rows[0:16], rows[16:32]
        even = jnp.where(low_half, a, pltpu.roll(b, CAP, 1))
        if j < 3:
            values.append(even)
            values.append(jnp.where(low_half, pltpu.roll(a, CAP, 1), b))
        else:
            cell = even.astype(I32)
    z, lane = place(cell)
    parts = [split(value) for value in values]
    row16 = lax.broadcasted_iota(I32, (16, 128), 0)
    row256 = lax.broadcasted_iota(I32, (256, 128), 0)
    for t in range(16):
        at = slice(t * 128, (t + 1) * 128)
        mine = row16 == z[t:t + 1]
        rhs[:, at] = jnp.where(row256 == lane[t:t + 1], 1.0, 0.0).astype(BF16)
        for k, (high, low) in enumerate(parts):
            lhs[k * 16:(k + 1) * 16, at] = jnp.where(mine, high[t:t + 1], 0.0).astype(BF16)
            lhs[96 + k * 16:96 + (k + 1) * 16, at] = jnp.where(mine, low[t:t + 1], 0.0).astype(BF16)
    sums = lax.dot_general(lhs[...], rhs[...], NT, preferred_element_type=F32)
    sums = sums[0:96] + sums[96:192]
    for k in range(6):
        for x in range(CX):
            leaving[k, x] = raw[k, x] + sums[k * 16:(k + 1) * 16, x * 128:(x + 1) * 128]


def count_rows(rows, counted, lhs, rhs):
    z, lane = place(rows[...])
    row16 = lax.broadcasted_iota(I32, (16, 128), 0)
    row256 = lax.broadcasted_iota(I32, (256, 128), 0)
    for t in range(16):
        at = slice(t * 128, (t + 1) * 128)
        lhs[0:16, at] = jnp.where(row16 == z[t:t + 1], 1.0, 0.0).astype(BF16)
        rhs[:, at] = jnp.where(row256 == lane[t:t + 1], 1.0, 0.0).astype(BF16)
    sums = lax.dot_general(lhs[0:16, :], rhs[...], NT, preferred_element_type=F32)
    for x in range(CX):
        counted[x] = sums[:, x * 128:(x + 1) * 128]


def place(cell):
    return (cell >> 7) & 15, ((cell >> 11) << 7) | (cell & 127)


def look_up(ids, tables, coefs):
    for m in range(2):
        for p in range(PX):
            block = ids[m, p]
            values = [jnp.zeros((RZ, CY), F32) for _ in tables]
            for entry in range(16):
                here = block == entry
                values = [jnp.where(here, table[entry], v) for table, v in zip(tables, values)]
            for k, v in enumerate(values):
                coefs[m, k, p] = 0.5 * v


def y_before(f, first):
    return jnp.where(first, 0.0, pltpu.roll(f, 1, 1))


def y_after(f, last):
    return jnp.where(last, 0.0, pltpu.roll(f, CY - 1, 1))


def z_before(f):
    return pltpu.roll(f, 1, 0)


def z_after(f):
    return pltpu.roll(f, RZ - 1, 0)


def increments(state, coefs, m, p):
    first = lax.broadcasted_iota(I32, (RZ, CY), 1) == 0
    b = coefs[m, 0, p]
    sxx, syy, szz, syz, sxz, sxy = (state[m, k, p] for k in range(3, 9))
    bxx, bxz, bxy = (state[m, k, p - 1] for k in (3, 7, 8))
    ix = b * ((sxx - bxx) + (sxy - y_before(sxy, first)) + (sxz - z_before(sxz)))
    iy = b * ((sxy - bxy) + (syy - y_before(syy, first)) + (syz - z_before(syz)))
    iz = b * ((sxz - bxz) + (syz - y_before(syz, first)) + (szz - z_before(szz)))
    return ix, iy, iz


def velocity(state, coefs, counts, planes):
    for p in planes:
        count = counts[p]
        regional, basin = increments(state, coefs, 0, p), increments(state, coefs, 1, p)
        for k in range(3):
            state[0, k, p] += regional[k]
            state[1, k, p] += basin[k] + count * regional[k]


def stress(state, coefs, planes):
    last = lax.broadcasted_iota(I32, (RZ, CY), 1) == CY - 1
    for m in range(2):
        for p in planes:
            lam, mu = coefs[m, 1, p], coefs[m, 2, p]
            vx, vy, vz = (state[m, k, p] for k in range(3))
            ax, ay, az = (state[m, k, p + 1] for k in range(3))
            exx = ax - vx
            eyy = y_after(vy, last) - vy
            ezz = z_after(vz) - vz
            bulk = lam * (exx + eyy + ezz)
            mu2 = mu + mu
            state[m, 3, p] += bulk + mu2 * exx
            state[m, 4, p] += bulk + mu2 * eyy
            state[m, 5, p] += bulk + mu2 * ezz
            state[m, 6, p] += mu * ((z_after(vy) - vy) + (y_after(vz, last) - vz))
            state[m, 7, p] += mu * ((z_after(vx) - vx) + (az - vz))
            state[m, 8, p] += mu * ((y_after(vx, last) - vx) + (ay - vy))


class Group:
    def __init__(self):
        self.copies = []

    def add(self, copy, sends, gets):
        self.copies.append((copy, sends, gets))

    def start(self):
        for copy, sends, _ in self.copies:
            pl.when(sends)(copy.start)

    def wait_recv(self):
        for copy, _, gets in self.copies:
            pl.when(gets)(copy.wait_recv)

    def wait_send(self):
        for copy, sends, _ in self.copies:
            pl.when(sends)(copy.wait_send)


def kernel(
    n_sec, n_depth, fields, block_ids, buoyancy, lame_lambda, lame_mu, moments, owners, cells, rows, out,
    staged, staged_ids, state, ids, counts, coefs, raw_stress, leaving, counted, to_right, to_left, from_left, from_right,
    owner_v, cells_v, rows_v, mom_v, bucket, arrived, lhs, rhs,
    local_sem, core_send, core_recv, raw_send, raw_recv, ids_send, ids_recv, count_send, count_recv, all_send, all_recv,
    first_send, first_recv, second_send, second_recv,
):
    sec, depth, seg = lax.axis_index("sec"), lax.axis_index("depth"), lax.axis_index("segment")
    partner = (sec, depth, 1 - seg)

    def load(k, src, dst):
        return pltpu.make_async_copy(src, dst, local_sem.at[k])

    def remote(src, dst, send, recv, to):
        return pltpu.make_async_remote_copy(
            src_ref=src, dst_ref=dst, send_sem=send, recv_sem=recv, device_id=to, device_id_type=MESH
        )

    def there(dx, dz):
        return in_range(sec + dx, depth + dz, n_sec, n_depth)

    loads = [load(0, owners, owner_v), load(1, cells, cells_v), load(2, moments, mom_v), load(3, rows, rows_v)]
    for copy in loads:
        copy.start()

    staged[...] = jnp.zeros_like(staged)
    staged_ids[...] = jnp.full_like(staged_ids, -1)
    state[0, 3:9] = jnp.zeros_like(state[0, 3:9])
    counts[...] = jnp.zeros_like(counts)
    if n_sec < BUCKETS:
        arrived[...] = jnp.zeros_like(arrived)

    barrier = pltpu.get_barrier_semaphore()
    expected = jnp.int32(n_sec)

    @pl.loop(1, n_sec)
    def _(j):
        pl.semaphore_signal(barrier, inc=1, device_id=(lax.rem(sec + j, n_sec), depth, seg), device_id_type=MESH)

    pl.semaphore_signal(barrier, inc=1, device_id=partner, device_id_type=MESH)
    for dx, dz in NEAR:
        if dz != 0:
            near = there(dx, dz)
            expected = expected + near.astype(I32)

            @pl.when(near)
            def _():
                pl.semaphore_signal(barrier, inc=1, device_id=(sec + dx, depth + dz, seg), device_id_type=MESH)

    own_state = load(4, fields.at[0], staged.at[:, OWN_X, rows_at(RIM, CZ)])
    own_ids = load(5, block_ids.at[0], staged_ids.at[OWN_X, rows_at(RIM, CZ)])
    own_stress = load(6, fields.at[0, 3:9], raw_stress)
    own_state.start()
    own_ids.start()
    pl.when(seg == 0)(own_stress.start)

    for copy in loads:
        copy.wait()
    fill_buckets(owner_v, cells_v, mom_v, bucket, lhs, rhs)

    pl.semaphore_wait(barrier, expected)

    def passed(j):
        to = lax.rem(sec + j, n_sec)
        return remote(
            bucket.at[lax.rem(to, 2) * 16 + to // 2], arrived.at[sec], all_send.at[j], all_recv.at[j], (to, depth, seg)
        )

    @pl.loop(0, n_sec - 1)
    def _(t):
        passed(1 + lax.rem(t + n_sec // 2 - 1, n_sec - 1)).start()

    arrived[sec] = bucket[lax.rem(sec, 2) * 16 + sec // 2]

    raw, raw_ids = Group(), Group()
    for q, (dx, dz) in enumerate(NEAR):
        from_z = {-1: rows_at(0, RIM), 0: rows_at(0, CZ), 1: rows_at(CZ - RIM, RIM)}[dz]
        to_z = {-1: rows_at(RIM + CZ, RIM), 0: rows_at(RIM, CZ), 1: rows_at(0, RIM)}[dz]
        to = (sec + dx, depth + dz, seg)
        sends, gets = there(dx, dz), there(-dx, -dz)
        for m, parts in ((0, slice(0, 3)), (1, slice(0, 9))):
            raw.add(
                remote(fields.at[0, parts, :, from_z], staged.at[parts, beside(dx), to_z], raw_send.at[q], raw_recv.at[q], to),
                jnp.logical_and(sends, seg == m), jnp.logical_and(gets, seg == m),
            )
        raw_ids.add(
            remote(block_ids.at[0, :, from_z], staged_ids.at[beside(dx), to_z], ids_send.at[q], ids_recv.at[q], to),
            sends, gets,
        )
    partner_stress = remote(fields.at[0, 3:9], raw_stress, core_send.at[0], core_recv.at[0], partner)
    raw_ids.start()
    pl.when(seg == 0)(partner_stress.start)
    raw.start()

    def window(source, target, send, recv):
        group = Group()
        for c in range(2):
            dz = 1 - 2 * c
            for q, (dx, goes) in enumerate(((-1, 0), (1, 0), (0, dz), (-1, dz), (1, dz))):
                if goes == 0:
                    from_z, to_z = rows_at(RIM * c, HZ + RIM), rows_at(RIM * (1 - c), HZ + RIM)
                else:
                    from_z, to_z = rows_at((CZ - RIM) * (1 - c), RIM), rows_at((HZ + RIM) * c, RIM)
                group.add(
                    remote(source(from_z), target(beside(dx), to_z), send.at[q], recv.at[q], (sec + dx, depth + goes, seg)),
                    jnp.logical_and(there(dx, goes), seg == c), jnp.logical_and(there(-dx, -goes), seg == c),
                )
        return group

    count_rows(rows_v, counted, lhs, rhs)
    for c in range(2):
        @pl.when(seg == c)
        def _():
            counts[OWN_X, rows_at(RIM * (1 - c), HZ + RIM)] = counted[:, rows_at(RIM * c, HZ + RIM)]

    near_counts = window(lambda z: counted.at[:, z], lambda x, z: counts.at[x, z], count_send, count_recv)
    near_counts.start()

    own_ids.wait()
    raw_ids.wait_recv()
    hand_ids, keep_ids, hand, keep = [], [], [], []
    for m, parts in ((0, slice(0, 3)), (1, slice(0, 9))):
        mine, theirs = rows_at(HZ * m, RZ), rows_at(HZ * (1 - m), RZ)
        hand_ids.append(remote(staged_ids.at[:, theirs], ids.at[m], core_send.at[1], core_recv.at[1], partner))
        keep_ids.append(load(7, staged_ids.at[:, mine], ids.at[m]))
        hand.append(remote(staged.at[parts, :, theirs], state.at[m, parts], core_send.at[2], core_recv.at[2], partner))
        keep.append(load(8, staged.at[parts, :, mine], state.at[m, parts]))

        @pl.when(seg == m)
        def _():
            hand_ids[m].start()
            keep_ids[m].start()

    own_state.wait()
    raw.wait_recv()
    for m in range(2):
        @pl.when(seg == m)
        def _():
            hand[m].start()
            keep[m].start()
    for m in range(2):
        @pl.when(seg == m)
        def _():
            keep_ids[m].wait()
            hand_ids[1 - m].wait_recv()
    look_up(ids, (buoyancy, lame_lambda, lame_mu), coefs)
    pl.when(seg == 0)(own_stress.wait)
    pl.when(seg == 1)(partner_stress.wait_recv)

    @pl.loop(1, n_sec)
    def _(j):
        come = lax.rem(sec + n_sec - j, n_sec)
        remote(bucket.at[0], arrived.at[come], all_send.at[j], all_recv.at[j], (come, depth, seg)).wait_recv()

    add_buckets(arrived, raw_stress, leaving, lhs, rhs)
    first = window(lambda z: leaving.at[:, :, z], lambda x, z: state.at[0, 3:9, x, z], first_send, first_recv)
    first.start()
    for c in range(2):
        @pl.when(seg == c)
        def _():
            state[0, 3:9, OWN_X, rows_at(RIM * (1 - c), HZ + RIM)] = leaving[:, :, rows_at(RIM * c, HZ + RIM)]

    for m in range(2):
        @pl.when(seg == m)
        def _():
            keep[m].wait()
            hand[1 - m].wait_recv()
    near_counts.wait_recv()
    first.wait_recv()

    lo, hi = X0, X0 + CX - 1
    velocity(state, coefs, counts, range(lo - 1, hi + 3))
    stress(state, coefs, range(lo - 1, hi + 2))
    velocity(state, coefs, counts, range(lo, hi + 2))
    stress(state, coefs, range(lo, hi + 1))
    velocity(state, coefs, counts, (hi,))
    for m in range(2):
        for k in range(3):
            to_right[m, k] = state[m, k, hi]
            to_left[m, k] = state[m, k, hi]
        for k, part in enumerate((3, 7, 8)):
            to_right[m, 3 + k] = state[m, part, hi]
        for k in range(3, 9):
            to_left[m, k] = state[m, k, lo]

    second = Group()
    z = rows_at(2, RZ - 4)
    for q, (dx, src, dst) in enumerate(((1, to_right, from_left), (-1, to_left, from_right))):
        second.add(
            remote(src.at[:, :, z], dst.at[:, :, z], second_send.at[q], second_recv.at[q], (sec + dx, depth, seg)),
            there(dx, 0), there(-dx, 0),
        )
    second.start()
    second.wait_recv()

    @pl.when(there(-1, 0))
    def _():
        for m in range(2):
            for k, part in enumerate((0, 1, 2, 3, 7, 8)):
                state[m, part, lo - 1] = from_left[m, k]

    @pl.when(there(1, 0))
    def _():
        for m in range(2):
            for k in range(3):
                state[m, k, hi + 2] = from_right[m, k]
            for k in range(3, 9):
                state[m, k, hi + 1] = from_right[m, k]

    velocity(state, coefs, counts, (lo, hi + 1))
    stress(state, coefs, range(lo - 1, hi + 2))
    velocity(state, coefs, counts, range(lo, hi + 2))
    stress(state, coefs, range(lo, hi + 1))

    results = []
    for c in range(2):
        part = rows_at(HZ * c, HZ)
        keeps = load(9, state.at[c, :, OWN_X, OWN_Z], out.at[0, :, :, part])
        gives = remote(state.at[1 - c, :, OWN_X, OWN_Z], out.at[0, :, :, part], core_send.at[3], core_recv.at[3], partner)
        results.append((keeps, gives))

        @pl.when(seg == c)
        def _():
            gives.start()
            keeps.start()

    for group in (raw, raw_ids, near_counts, first, second):
        group.wait_send()
    pl.when(seg == 0)(partner_stress.wait_send)
    for c in range(2):
        @pl.when(seg == c)
        def _():
            hand_ids[c].wait_send()
            hand[c].wait_send()

    @pl.loop(1, n_sec)
    def _(j):
        passed(j).wait_send()

    for c in range(2):
        @pl.when(seg == c)
        def _():
            results[c][0].wait()
            results[c][1].wait_send()
            results[1 - c][1].wait_recv()


def on_device(
    n_sec, n_depth, fields, block_ids, buoyancy, lame_lambda, lame_mu, moments, moment_owner, moment_cells, drm_rows
):
    owners = moment_owner.reshape(ENT // 128, 128)
    cells = moment_cells.reshape(ENT // 128, 128)
    rows = drm_rows.reshape(ROWS // 128, 128)
    hbm = pl.BlockSpec(memory_space=pl.ANY)
    smem = pl.BlockSpec(memory_space=pltpu.SMEM)
    dma = pltpu.SemaphoreType.DMA
    vmem = pltpu.VMEM
    return pl.pallas_call(
        functools.partial(kernel, n_sec, n_depth),
        out_shape=jax.ShapeDtypeStruct(fields.shape, F32),
        in_specs=[hbm, hbm, smem, smem, smem, hbm, hbm, hbm, hbm],
        out_specs=hbm,
        scratch_shapes=[
            vmem((9, PX, GZ, CY), F32),
            vmem((PX, GZ, CY), I32),
            vmem((2, 9, PX, RZ, CY), F32),
            vmem((2, PX, RZ, CY), I32),
            vmem((PX, RZ, CY), F32),
            vmem((2, 3, PX, RZ, CY), F32),
            vmem((6, CX, CZ, CY), F32),
            vmem((6, CX, CZ, CY), F32),
            vmem((CX, CZ, CY), F32),
            vmem((2, 6, RZ, CY), F32),
            vmem((2, 9, RZ, CY), F32),
            vmem((2, 6, RZ, CY), F32),
            vmem((2, 9, RZ, CY), F32),
            vmem((ENT // 128, 128), I32),
            vmem((ENT // 128, 128), I32),
            vmem((ROWS // 128, 128), I32),
            vmem((6, ENT), F32),
            vmem((BUCKETS, 4, 128), F32),
            vmem((BUCKETS, 4, 128), F32),
            vmem((192, 2048), BF16),
            vmem((256, 2048), BF16),
            dma((10,)),
            dma((4,)), dma((4,)),
            dma((8,)), dma((8,)),
            dma((8,)), dma((8,)),
            dma((5,)), dma((5,)),
            dma((BUCKETS,)), dma((BUCKETS,)),
            dma((5,)), dma((5,)),
            dma((2,)), dma((2,)),
        ],
        compiler_params=pltpu.CompilerParams(collective_id=0, has_side_effects=True),
    )(fields, block_ids, buoyancy, lame_lambda, lame_mu, moments, owners, cells, rows)


def solution(mesh):
    in_specs = (
        P("segment", None, "sec", "depth", None),
        P("segment", "sec", "depth", None),
        P(),
        P(),
        P(),
        P(None, ("sec", "depth")),
        P(("sec", "depth"), None),
        P(("sec", "depth")),
        P(("sec", "depth")),
    )
    return jax.shard_map(
        functools.partial(on_device, mesh.shape["sec"], mesh.shape["depth"]),
        mesh=mesh, in_specs=in_specs, out_specs=P("segment", None, "sec", "depth", None), check_vma=False,
    )
```

```python
import functools

import jax
import jax.numpy as jnp
from jax import lax
from jax.experimental import pallas as pl
from jax.experimental.pallas import tpu as pltpu
from jax.sharding import PartitionSpec as P

MESH = pl.DeviceIdType.MESH
CX, CZ, CY = 2, 16, 128
ENT, ROWS, CAP, BUCKETS = 1024, 2048, 64, 32
HZ, RIM = CZ // 2, 4
PX, RZ, GZ = CX + 4, HZ + 2 * RIM, CZ + 2 * RIM
X0 = 2
OWN_X, OWN_Z = slice(X0, X0 + CX), slice(RIM, RIM + HZ)
NEAR = tuple((dx, dz) for dx in (-1, 0, 1) for dz in (-1, 0, 1) if (dx, dz) != (0, 0))
NT = (((1,), (1,)), ((), ()))
BF16, F32, I32 = jnp.bfloat16, jnp.float32, jnp.int32


def split(value):
    high = value.astype(BF16).astype(F32)
    return high, value - high


def rows_at(start, size):
    return slice(start, start + size)


def beside(dx):
    return rows_at(X0 - CX * dx, CX)


def in_range(sec, depth, n_sec, n_depth):
    ok_sec = jnp.logical_and(sec >= 0, sec < n_sec)
    ok_depth = jnp.logical_and(depth >= 0, depth < n_depth)
    return jnp.logical_and(ok_sec, ok_depth)


def fill_buckets(owner, cells, mom, bucket, lhs, rhs):
    owners = [owner[t:t + 1, :] for t in range(8)]
    row32 = lax.broadcasted_iota(I32, (BUCKETS, 128), 0)
    hot = [jnp.where(row32 == o, 1.0, 0.0) for o in owners]
    before = jnp.where(
        lax.broadcasted_iota(I32, (128, 256), 0) < lax.broadcasted_iota(I32, (128, 256), 1), 1.0, 0.0
    ).astype(BF16)
    counts = jnp.dot(jnp.concatenate(hot, 0).astype(BF16), before, preferred_element_type=F32)
    running = jnp.zeros((BUCKETS, 128), F32)
    row16 = lax.broadcasted_iota(I32, (16, 128), 0)
    row256 = lax.broadcasted_iota(I32, (256, 128), 0)
    for t in range(8):
        part = counts[t * BUCKETS:(t + 1) * BUCKETS]
        rank = jnp.sum(hot[t] * (part[:, :128] + running), axis=0, keepdims=True).astype(I32)
        running = running + part[:, 128:]
        cols = slice(t * 128, (t + 1) * 128)
        slot = (owners[t] & 1) * 128 + rank
        mine = row16 == (owners[t] >> 1)
        cell = cells[t:t + 1, :].astype(F32)
        for h in range(2):
            at = slice((2 * t + h) * 128, (2 * t + h + 1) * 128)
            rhs[:, at] = jnp.where(row256 == slot + h * CAP, 1.0, 0.0).astype(BF16)
            for j in range(4):
                value = mom[2 * j + h:2 * j + h + 1, cols] if j < 3 else cell
                high, low = split(value)
                lhs[j * 16:(j + 1) * 16, at] = jnp.where(mine, high, 0.0).astype(BF16)
                lhs[64 + j * 16:64 + (j + 1) * 16, at] = jnp.where(mine, low, 0.0).astype(BF16)
    sums = lax.dot_general(lhs[0:128, :], rhs[...], NT, preferred_element_type=F32)
    sums = sums[0:64] + sums[64:128]
    for j in range(4):
        for x in range(2):
            bucket[x * 16:(x + 1) * 16, j, :] = sums[j * 16:(j + 1) * 16, x * 128:(x + 1) * 128]


def place(cell):
    return (cell >> 7) & 15, ((cell >> 11) << 7) | (cell & 127)


def add_buckets(arrived, raw, leaving, lhs, rhs):
    low_half = lax.broadcasted_iota(I32, (16, 128), 1) < CAP
    values, cell = [], None
    for j in range(4):
        rows = arrived[:, j, :]
        a, b = rows[0:16], rows[16:32]
        even = jnp.where(low_half, a, pltpu.roll(b, CAP, 1))
        if j < 3:
            values.append(even)
            values.append(jnp.where(low_half, pltpu.roll(a, CAP, 1), b))
        else:
            cell = even.astype(I32)
    z, lane = place(cell)
    parts = [split(value) for value in values]
    row16 = lax.broadcasted_iota(I32, (16, 128), 0)
    row256 = lax.broadcasted_iota(I32, (256, 128), 0)
    for t in range(16):
        at = slice(t * 128, (t + 1) * 128)
        mine = row16 == z[t:t + 1]
        rhs[:, at] = jnp.where(row256 == lane[t:t + 1], 1.0, 0.0).astype(BF16)
        for k, (high, low) in enumerate(parts):
            lhs[k * 16:(k + 1) * 16, at] = jnp.where(mine, high[t:t + 1], 0.0).astype(BF16)
            lhs[96 + k * 16:96 + (k + 1) * 16, at] = jnp.where(mine, low[t:t + 1], 0.0).astype(BF16)
    sums = lax.dot_general(lhs[...], rhs[...], NT, preferred_element_type=F32)
    sums = sums[0:96] + sums[96:192]
    for k in range(6):
        for x in range(CX):
            leaving[k, x] = raw[k, x] + sums[k * 16:(k + 1) * 16, x * 128:(x + 1) * 128]


def count_rows(rows, counted, lhs, rhs):
    z, lane = place(rows[...])
    row16 = lax.broadcasted_iota(I32, (16, 128), 0)
    row256 = lax.broadcasted_iota(I32, (256, 128), 0)
    for t in range(16):
        at = slice(t * 128, (t + 1) * 128)
        lhs[0:16, at] = jnp.where(row16 == z[t:t + 1], 1.0, 0.0).astype(BF16)
        rhs[:, at] = jnp.where(row256 == lane[t:t + 1], 1.0, 0.0).astype(BF16)
    sums = lax.dot_general(lhs[0:16, :], rhs[...], NT, preferred_element_type=F32)
    for x in range(CX):
        counted[x] = sums[:, x * 128:(x + 1) * 128]


def place(cell):
    return (cell >> 7) & 15, ((cell >> 11) << 7) | (cell & 127)


def look_up(ids, tables, coefs):
    for m in range(2):
        for p in range(PX):
            block = ids[m, p]
            values = [jnp.zeros((RZ, CY), F32) for _ in range(3)]
            for entry in range(16):
                here = block == entry
                values = [jnp.where(here, tables[k, entry], v) for k, v in enumerate(values)]
            for k, v in enumerate(values):
                coefs[m, k, p] = 0.5 * v


def y_before(f, first):
    return jnp.where(first, 0.0, pltpu.roll(f, 1, 1))


def y_after(f, last):
    return jnp.where(last, 0.0, pltpu.roll(f, CY - 1, 1))


def z_before(f):
    return pltpu.roll(f, 1, 0)


def z_after(f):
    return pltpu.roll(f, RZ - 1, 0)


def increments(state, coefs, m, p):
    first = lax.broadcasted_iota(I32, (RZ, CY), 1) == 0
    b = coefs[m, 0, p]
    sxx, syy, szz, syz, sxz, sxy = (state[m, k, p] for k in range(3, 9))
    bxx, bxz, bxy = (state[m, k, p - 1] for k in (3, 7, 8))
    ix = b * ((sxx - bxx) + (sxy - y_before(sxy, first)) + (sxz - z_before(sxz)))
    iy = b * ((sxy - bxy) + (syy - y_before(syy, first)) + (syz - z_before(syz)))
    iz = b * ((sxz - bxz) + (syz - y_before(syz, first)) + (szz - z_before(szz)))
    return ix, iy, iz


def velocity(state, coefs, counts, planes):
    for p in planes:
        count = counts[p]
        regional, basin = increments(state, coefs, 0, p), increments(state, coefs, 1, p)
        for k in range(3):
            state[0, k, p] += regional[k]
            state[1, k, p] += basin[k] + count * regional[k]


def stress(state, coefs, planes):
    last = lax.broadcasted_iota(I32, (RZ, CY), 1) == CY - 1
    for m in range(2):
        for p in planes:
            lam, mu = coefs[m, 1, p], coefs[m, 2, p]
            vx, vy, vz = (state[m, k, p] for k in range(3))
            ax, ay, az = (state[m, k, p + 1] for k in range(3))
            exx = ax - vx
            eyy = y_after(vy, last) - vy
            ezz = z_after(vz) - vz
            bulk = lam * (exx + eyy + ezz)
            mu2 = mu + mu
            state[m, 3, p] += bulk + mu2 * exx
            state[m, 4, p] += bulk + mu2 * eyy
            state[m, 5, p] += bulk + mu2 * ezz
            state[m, 6, p] += mu * ((z_after(vy) - vy) + (y_after(vz, last) - vz))
            state[m, 7, p] += mu * ((z_after(vx) - vx) + (az - vz))
            state[m, 8, p] += mu * ((y_after(vx, last) - vx) + (ay - vy))


class Group:
    def __init__(self):
        self.copies = []

    def add(self, copy, sends, gets):
        self.copies.append((copy, sends, gets))

    def start(self):
        for copy, sends, _ in self.copies:
            pl.when(sends)(copy.start)

    def wait_recv(self):
        for copy, _, gets in self.copies:
            pl.when(gets)(copy.wait_recv)

    def wait_send(self):
        for copy, sends, _ in self.copies:
            pl.when(sends)(copy.wait_send)


def kernel(
    n_sec, n_depth, fields, block_ids, buoyancy, lame_lambda, lame_mu, moments, owners, cells, rows, out,
    tables, staged, staged_ids, state, ids, counts, coefs, raw_stress, leaving, counted, to_right, to_left, from_left, from_right,
    owner_v, cells_v, rows_v, mom_v, bucket, arrived, lhs, rhs,
    local_sem, core_send, core_recv, raw_send, raw_recv, ids_send, ids_recv, count_send, count_recv, all_send, all_recv,
    first_send, first_recv, second_send, second_recv,
):
    sec, depth, seg = lax.axis_index("sec"), lax.axis_index("depth"), lax.axis_index("segment")
    partner = (sec, depth, 1 - seg)

    def load(k, src, dst):
        return pltpu.make_async_copy(src, dst, local_sem.at[k])

    def remote(src, dst, send, recv, to):
        return pltpu.make_async_remote_copy(
            src_ref=src, dst_ref=dst, send_sem=send, recv_sem=recv, device_id=to, device_id_type=MESH
        )

    def there(dx, dz):
        return in_range(sec + dx, depth + dz, n_sec, n_depth)

    loads = [load(0, owners, owner_v), load(1, cells, cells_v), load(2, moments, mom_v), load(3, rows, rows_v)]
    table_loads = [load(10 + k, table, tables.at[k]) for k, table in enumerate((buoyancy, lame_lambda, lame_mu))]
    for copy in loads + table_loads:
        copy.start()

    staged[...] = jnp.zeros_like(staged)
    staged_ids[...] = jnp.full_like(staged_ids, -1)
    state[0, 3:9] = jnp.zeros_like(state[0, 3:9])
    counts[...] = jnp.zeros_like(counts)
    if n_sec < BUCKETS:
        arrived[...] = jnp.zeros_like(arrived)

    barrier = pltpu.get_barrier_semaphore()
    expected = jnp.int32(n_sec)

    @pl.loop(1, n_sec)
    def _(j):
        pl.semaphore_signal(barrier, inc=1, device_id=(lax.rem(sec + j, n_sec), depth, seg), device_id_type=MESH)

    pl.semaphore_signal(barrier, inc=1, device_id=partner, device_id_type=MESH)
    for dx, dz in NEAR:
        if dz != 0:
            near = there(dx, dz)
            expected = expected + near.astype(I32)

            @pl.when(near)
            def _():
                pl.semaphore_signal(barrier, inc=1, device_id=(sec + dx, depth + dz, seg), device_id_type=MESH)

    own_state = load(4, fields.at[0], staged.at[:, OWN_X, rows_at(RIM, CZ)])
    own_ids = load(5, block_ids.at[0], staged_ids.at[OWN_X, rows_at(RIM, CZ)])
    own_stress = load(6, fields.at[0, 3:9], raw_stress)
    own_state.start()
    own_ids.start()
    pl.when(seg == 0)(own_stress.start)

    for copy in loads:
        copy.wait()
    fill_buckets(owner_v, cells_v, mom_v, bucket, lhs, rhs)

    pl.semaphore_wait(barrier, expected)

    def passed(j):
        to = lax.rem(sec + j, n_sec)
        return remote(
            bucket.at[lax.rem(to, 2) * 16 + to // 2], arrived.at[sec], all_send.at[j], all_recv.at[j], (to, depth, seg)
        )

    @pl.loop(0, n_sec - 1)
    def _(t):
        passed(1 + lax.rem(t + n_sec // 2 - 1, n_sec - 1)).start()

    arrived[sec] = bucket[lax.rem(sec, 2) * 16 + sec // 2]

    raw, raw_ids = Group(), Group()
    for q, (dx, dz) in enumerate(NEAR):
        from_z = {-1: rows_at(0, RIM), 0: rows_at(0, CZ), 1: rows_at(CZ - RIM, RIM)}[dz]
        to_z = {-1: rows_at(RIM + CZ, RIM), 0: rows_at(RIM, CZ), 1: rows_at(0, RIM)}[dz]
        to = (sec + dx, depth + dz, seg)
        sends, gets = there(dx, dz), there(-dx, -dz)
        for m, parts in ((0, slice(0, 3)), (1, slice(0, 9))):
            raw.add(
                remote(fields.at[0, parts, :, from_z], staged.at[parts, beside(dx), to_z], raw_send.at[q], raw_recv.at[q], to),
                jnp.logical_and(sends, seg == m), jnp.logical_and(gets, seg == m),
            )
        raw_ids.add(
            remote(block_ids.at[0, :, from_z], staged_ids.at[beside(dx), to_z], ids_send.at[q], ids_recv.at[q], to),
            sends, gets,
        )
    partner_stress = remote(fields.at[0, 3:9], raw_stress, core_send.at[0], core_recv.at[0], partner)
    raw_ids.start()
    pl.when(seg == 0)(partner_stress.start)
    raw.start()

    def window(source, target, send, recv):
        group = Group()
        for c in range(2):
            dz = 1 - 2 * c
            for q, (dx, goes) in enumerate(((-1, 0), (1, 0), (0, dz), (-1, dz), (1, dz))):
                if goes == 0:
                    from_z, to_z = rows_at(RIM * c, HZ + RIM), rows_at(RIM * (1 - c), HZ + RIM)
                else:
                    from_z, to_z = rows_at((CZ - RIM) * (1 - c), RIM), rows_at((HZ + RIM) * c, RIM)
                group.add(
                    remote(source(from_z), target(beside(dx), to_z), send.at[q], recv.at[q], (sec + dx, depth + goes, seg)),
                    jnp.logical_and(there(dx, goes), seg == c), jnp.logical_and(there(-dx, -goes), seg == c),
                )
        return group

    count_rows(rows_v, counted, lhs, rhs)
    for c in range(2):
        @pl.when(seg == c)
        def _():
            counts[OWN_X, rows_at(RIM * (1 - c), HZ + RIM)] = counted[:, rows_at(RIM * c, HZ + RIM)]

    near_counts = window(lambda z: counted.at[:, z], lambda x, z: counts.at[x, z], count_send, count_recv)
    near_counts.start()

    pl.when(seg == 0)(own_stress.wait)
    pl.when(seg == 1)(partner_stress.wait_recv)

    @pl.loop(1, n_sec)
    def _(j):
        come = lax.rem(sec + n_sec - j, n_sec)
        remote(bucket.at[0], arrived.at[come], all_send.at[j], all_recv.at[j], (come, depth, seg)).wait_recv()

    add_buckets(arrived, raw_stress, leaving, lhs, rhs)
    first = window(lambda z: leaving.at[:, :, z], lambda x, z: state.at[0, 3:9, x, z], first_send, first_recv)
    first.start()
    for c in range(2):
        @pl.when(seg == c)
        def _():
            state[0, 3:9, OWN_X, rows_at(RIM * (1 - c), HZ + RIM)] = leaving[:, :, rows_at(RIM * c, HZ + RIM)]

    own_ids.wait()
    raw_ids.wait_recv()
    hand_ids, keep_ids, hand, keep = [], [], [], []
    for m, parts in ((0, slice(0, 3)), (1, slice(0, 9))):
        mine, theirs = rows_at(HZ * m, RZ), rows_at(HZ * (1 - m), RZ)
        hand_ids.append(remote(staged_ids.at[:, theirs], ids.at[m], core_send.at[1], core_recv.at[1], partner))
        keep_ids.append(load(7, staged_ids.at[:, mine], ids.at[m]))
        hand.append(remote(staged.at[parts, :, theirs], state.at[m, parts], core_send.at[2], core_recv.at[2], partner))
        keep.append(load(8, staged.at[parts, :, mine], state.at[m, parts]))

        @pl.when(seg == m)
        def _():
            hand_ids[m].start()
            keep_ids[m].start()

    own_state.wait()
    raw.wait_recv()
    for m in range(2):
        @pl.when(seg == m)
        def _():
            hand[m].start()
            keep[m].start()
    for m in range(2):
        @pl.when(seg == m)
        def _():
            keep_ids[m].wait()
            hand_ids[1 - m].wait_recv()
    for copy in table_loads:
        copy.wait()
    look_up(ids, tables, coefs)
    for m in range(2):
        @pl.when(seg == m)
        def _():
            keep[m].wait()
            hand[1 - m].wait_recv()
    near_counts.wait_recv()
    first.wait_recv()

    lo, hi = X0, X0 + CX - 1
    velocity(state, coefs, counts, range(lo - 1, hi + 3))
    stress(state, coefs, range(lo - 1, hi + 2))
    velocity(state, coefs, counts, range(lo, hi + 2))
    stress(state, coefs, range(lo, hi + 1))
    velocity(state, coefs, counts, (hi,))
    for m in range(2):
        for k in range(3):
            to_right[m, k] = state[m, k, hi]
            to_left[m, k] = state[m, k, hi]
        for k, part in enumerate((3, 7, 8)):
            to_right[m, 3 + k] = state[m, part, hi]
        for k in range(3, 9):
            to_left[m, k] = state[m, k, lo]

    second = Group()
    z = rows_at(2, RZ - 4)
    for q, (dx, src, dst) in enumerate(((1, to_right, from_left), (-1, to_left, from_right))):
        second.add(
            remote(src.at[:, :, z], dst.at[:, :, z], second_send.at[q], second_recv.at[q], (sec + dx, depth, seg)),
            there(dx, 0), there(-dx, 0),
        )
    second.start()
    second.wait_recv()

    @pl.when(there(-1, 0))
    def _():
        for m in range(2):
            for k, part in enumerate((0, 1, 2, 3, 7, 8)):
                state[m, part, lo - 1] = from_left[m, k]

    @pl.when(there(1, 0))
    def _():
        for m in range(2):
            for k in range(3):
                state[m, k, hi + 2] = from_right[m, k]
            for k in range(3, 9):
                state[m, k, hi + 1] = from_right[m, k]

    velocity(state, coefs, counts, (lo, hi + 1))
    stress(state, coefs, range(lo - 1, hi + 2))
    velocity(state, coefs, counts, range(lo, hi + 2))
    stress(state, coefs, range(lo, hi + 1))

    results = []
    for c in range(2):
        part = rows_at(HZ * c, HZ)
        keeps = load(9, state.at[c, :, OWN_X, OWN_Z], out.at[0, :, :, part])
        gives = remote(state.at[1 - c, :, OWN_X, OWN_Z], out.at[0, :, :, part], core_send.at[3], core_recv.at[3], partner)
        results.append((keeps, gives))

        @pl.when(seg == c)
        def _():
            gives.start()
            keeps.start()

    for group in (raw, raw_ids, near_counts, first, second):
        group.wait_send()
    pl.when(seg == 0)(partner_stress.wait_send)
    for c in range(2):
        @pl.when(seg == c)
        def _():
            hand_ids[c].wait_send()
            hand[c].wait_send()

    @pl.loop(1, n_sec)
    def _(j):
        passed(j).wait_send()

    for c in range(2):
        @pl.when(seg == c)
        def _():
            results[c][0].wait()
            results[c][1].wait_send()
            results[1 - c][1].wait_recv()


def on_device(
    n_sec, n_depth, fields, block_ids, buoyancy, lame_lambda, lame_mu, moments, moment_owner, moment_cells, drm_rows
):
    owners = moment_owner.reshape(ENT // 128, 128)
    cells = moment_cells.reshape(ENT // 128, 128)
    rows = drm_rows.reshape(ROWS // 128, 128)
    hbm = pl.BlockSpec(memory_space=pl.ANY)
    dma = pltpu.SemaphoreType.DMA
    vmem = pltpu.VMEM
    return pl.pallas_call(
        functools.partial(kernel, n_sec, n_depth),
        out_shape=pltpu.VMEM(fields.shape, F32),
        in_specs=[hbm] * 9,
        out_specs=pl.BlockSpec(memory_space=pltpu.VMEM),
        scratch_shapes=[
            pltpu.SMEM((3, 16), F32),
            vmem((9, PX, GZ, CY), F32),
            vmem((PX, GZ, CY), I32),
            vmem((2, 9, PX, RZ, CY), F32),
            vmem((2, PX, RZ, CY), I32),
            vmem((PX, RZ, CY), F32),
            vmem((2, 3, PX, RZ, CY), F32),
            vmem((6, CX, CZ, CY), F32),
            vmem((6, CX, CZ, CY), F32),
            vmem((CX, CZ, CY), F32),
            vmem((2, 6, RZ, CY), F32),
            vmem((2, 9, RZ, CY), F32),
            vmem((2, 6, RZ, CY), F32),
            vmem((2, 9, RZ, CY), F32),
            vmem((ENT // 128, 128), I32),
            vmem((ENT // 128, 128), I32),
            vmem((ROWS // 128, 128), I32),
            vmem((6, ENT), F32),
            vmem((BUCKETS, 4, 128), F32),
            vmem((BUCKETS, 4, 128), F32),
            vmem((192, 2048), BF16),
            vmem((256, 2048), BF16),
            dma((13,)),
            dma((4,)), dma((4,)),
            dma((8,)), dma((8,)),
            dma((8,)), dma((8,)),
            dma((5,)), dma((5,)),
            dma((BUCKETS,)), dma((BUCKETS,)),
            dma((5,)), dma((5,)),
            dma((2,)), dma((2,)),
        ],
        compiler_params=pltpu.CompilerParams(collective_id=0, has_side_effects=True),
    )(fields, block_ids, buoyancy, lame_lambda, lame_mu, moments, owners, cells, rows)


def solution(mesh):
    in_specs = (
        P("segment", None, "sec", "depth", None),
        P("segment", "sec", "depth", None),
        P(),
        P(),
        P(),
        P(None, ("sec", "depth")),
        P(("sec", "depth"), None),
        P(("sec", "depth")),
        P(("sec", "depth")),
    )
    return jax.shard_map(
        functools.partial(on_device, mesh.shape["sec"], mesh.shape["depth"]),
        mesh=mesh, in_specs=in_specs, out_specs=P("segment", None, "sec", "depth", None), check_vma=False,
    )
```

```python
import functools

import jax
import jax.numpy as jnp
from jax import lax
from jax.experimental import pallas as pl
from jax.experimental.pallas import tpu as pltpu
from jax.sharding import PartitionSpec as P

MESH = pl.DeviceIdType.MESH
CX, CZ, CY = 2, 16, 128
ENT, ROWS, CAP, BUCKETS = 1024, 2048, 64, 32
HZ, RIM = CZ // 2, 4
PX, RZ, GZ = CX + 4, HZ + 2 * RIM, CZ + 2 * RIM
X0 = 2
OWN_X, OWN_Z = slice(X0, X0 + CX), slice(RIM, RIM + HZ)
NEAR = tuple((dx, dz) for dx in (-1, 0, 1) for dz in (-1, 0, 1) if (dx, dz) != (0, 0))
NT = (((1,), (1,)), ((), ()))
BF16, F32, I32 = jnp.bfloat16, jnp.float32, jnp.int32


def split(value):
    high = value.astype(BF16).astype(F32)
    return high, value - high


def rows_at(start, size):
    return slice(start, start + size)


def beside(dx):
    return rows_at(X0 - CX * dx, CX)


def in_range(sec, depth, n_sec, n_depth):
    ok_sec = jnp.logical_and(sec >= 0, sec < n_sec)
    ok_depth = jnp.logical_and(depth >= 0, depth < n_depth)
    return jnp.logical_and(ok_sec, ok_depth)


def fill_buckets(owner, cells, mom, bucket, lhs, rhs):
    owners = [owner[t:t + 1, :] for t in range(8)]
    row32 = lax.broadcasted_iota(I32, (BUCKETS, 128), 0)
    hot = [jnp.where(row32 == o, 1.0, 0.0) for o in owners]
    before = jnp.where(
        lax.broadcasted_iota(I32, (128, 256), 0) < lax.broadcasted_iota(I32, (128, 256), 1), 1.0, 0.0
    ).astype(BF16)
    counts = jnp.dot(jnp.concatenate(hot, 0).astype(BF16), before, preferred_element_type=F32)
    running = jnp.zeros((BUCKETS, 128), F32)
    row16 = lax.broadcasted_iota(I32, (16, 128), 0)
    row256 = lax.broadcasted_iota(I32, (256, 128), 0)
    for t in range(8):
        part = counts[t * BUCKETS:(t + 1) * BUCKETS]
        rank = jnp.sum(hot[t] * (part[:, :128] + running), axis=0, keepdims=True).astype(I32)
        running = running + part[:, 128:]
        cols = slice(t * 128, (t + 1) * 128)
        slot = (owners[t] & 1) * 128 + rank
        mine = row16 == (owners[t] >> 1)
        cell = cells[t:t + 1, :].astype(F32)
        for h in range(2):
            at = slice((2 * t + h) * 128, (2 * t + h + 1) * 128)
            rhs[:, at] = jnp.where(row256 == slot + h * CAP, 1.0, 0.0).astype(BF16)
            for j in range(4):
                value = mom[2 * j + h:2 * j + h + 1, cols] if j < 3 else cell
                high, low = split(value)
                lhs[j * 16:(j + 1) * 16, at] = jnp.where(mine, high, 0.0).astype(BF16)
                lhs[64 + j * 16:64 + (j + 1) * 16, at] = jnp.where(mine, low, 0.0).astype(BF16)
    sums = lax.dot_general(lhs[0:128, :], rhs[...], NT, preferred_element_type=F32)
    sums = sums[0:64] + sums[64:128]
    for j in range(4):
        for x in range(2):
            bucket[x * 16:(x + 1) * 16, j, :] = sums[j * 16:(j + 1) * 16, x * 128:(x + 1) * 128]


def place(cell):
    return (cell >> 7) & 15, ((cell >> 11) << 7) | (cell & 127)


def by_distance(n_sec):
    def hops(offset):
        row, col = offset // 4, offset % 4
        return min(row, n_sec // 4 - row) + min(col, 4 - col)

    return sorted(range(1, n_sec), key=hops)


def spread_buckets(arrived, batch, lhs, rhs):
    low_half = lax.broadcasted_iota(I32, (8, 128), 1) < CAP
    values, cell = [], None
    for j in range(4):
        a, b = arrived[batch * 16:batch * 16 + 8, j, :], arrived[batch * 16 + 8:batch * 16 + 16, j, :]
        even = jnp.where(low_half, a, pltpu.roll(b, CAP, 1))
        if j < 3:
            values.append(even)
            values.append(jnp.where(low_half, pltpu.roll(a, CAP, 1), b))
        else:
            cell = even.astype(I32)
    z, lane = place(cell)
    parts = [split(value) for value in values]
    row16 = lax.broadcasted_iota(I32, (16, 128), 0)
    row256 = lax.broadcasted_iota(I32, (256, 128), 0)
    half = slice(batch * 1024, (batch + 1) * 1024)
    for t in range(8):
        at = slice(batch * 1024 + t * 128, batch * 1024 + (t + 1) * 128)
        mine = row16 == z[t:t + 1]
        rhs[:, at] = jnp.where(row256 == lane[t:t + 1], 1.0, 0.0).astype(BF16)
        for k, (high, low) in enumerate(parts):
            lhs[k * 16:(k + 1) * 16, at] = jnp.where(mine, high[t:t + 1], 0.0).astype(BF16)
            lhs[96 + k * 16:96 + (k + 1) * 16, at] = jnp.where(mine, low[t:t + 1], 0.0).astype(BF16)
    sums = lax.dot_general(lhs[:, half], rhs[:, half], NT, preferred_element_type=F32)
    return sums[0:96] + sums[96:192]


def count_rows(rows, counted, lhs, rhs):
    z, lane = place(rows[...])
    row16 = lax.broadcasted_iota(I32, (16, 128), 0)
    row256 = lax.broadcasted_iota(I32, (256, 128), 0)
    for t in range(16):
        at = slice(t * 128, (t + 1) * 128)
        lhs[0:16, at] = jnp.where(row16 == z[t:t + 1], 1.0, 0.0).astype(BF16)
        rhs[:, at] = jnp.where(row256 == lane[t:t + 1], 1.0, 0.0).astype(BF16)
    sums = lax.dot_general(lhs[0:16, :], rhs[...], NT, preferred_element_type=F32)
    for x in range(CX):
        counted[x] = sums[:, x * 128:(x + 1) * 128]


def place(cell):
    return (cell >> 7) & 15, ((cell >> 11) << 7) | (cell & 127)


def look_up(ids, tables, coefs):
    for m in range(2):
        for p in range(PX):
            block = ids[m, p]
            values = [jnp.zeros((RZ, CY), F32) for _ in range(3)]
            for entry in range(16):
                here = block == entry
                values = [jnp.where(here, tables[k, entry], v) for k, v in enumerate(values)]
            for k, v in enumerate(values):
                coefs[m, k, p] = 0.5 * v


def y_before(f, first):
    return jnp.where(first, 0.0, pltpu.roll(f, 1, 1))


def y_after(f, last):
    return jnp.where(last, 0.0, pltpu.roll(f, CY - 1, 1))


def z_before(f):
    return pltpu.roll(f, 1, 0)


def z_after(f):
    return pltpu.roll(f, RZ - 1, 0)


def increments(state, coefs, m, p):
    first = lax.broadcasted_iota(I32, (RZ, CY), 1) == 0
    b = coefs[m, 0, p]
    sxx, syy, szz, syz, sxz, sxy = (state[m, k, p] for k in range(3, 9))
    bxx, bxz, bxy = (state[m, k, p - 1] for k in (3, 7, 8))
    ix = b * ((sxx - bxx) + (sxy - y_before(sxy, first)) + (sxz - z_before(sxz)))
    iy = b * ((sxy - bxy) + (syy - y_before(syy, first)) + (syz - z_before(syz)))
    iz = b * ((sxz - bxz) + (syz - y_before(syz, first)) + (szz - z_before(szz)))
    return ix, iy, iz


def velocity(state, coefs, counts, planes):
    for p in planes:
        count = counts[p]
        regional, basin = increments(state, coefs, 0, p), increments(state, coefs, 1, p)
        for k in range(3):
            state[0, k, p] += regional[k]
            state[1, k, p] += basin[k] + count * regional[k]


def stress(state, coefs, planes):
    last = lax.broadcasted_iota(I32, (RZ, CY), 1) == CY - 1
    for m in range(2):
        for p in planes:
            lam, mu = coefs[m, 1, p], coefs[m, 2, p]
            vx, vy, vz = (state[m, k, p] for k in range(3))
            ax, ay, az = (state[m, k, p + 1] for k in range(3))
            exx = ax - vx
            eyy = y_after(vy, last) - vy
            ezz = z_after(vz) - vz
            bulk = lam * (exx + eyy + ezz)
            mu2 = mu + mu
            state[m, 3, p] += bulk + mu2 * exx
            state[m, 4, p] += bulk + mu2 * eyy
            state[m, 5, p] += bulk + mu2 * ezz
            state[m, 6, p] += mu * ((z_after(vy) - vy) + (y_after(vz, last) - vz))
            state[m, 7, p] += mu * ((z_after(vx) - vx) + (az - vz))
            state[m, 8, p] += mu * ((y_after(vx, last) - vx) + (ay - vy))


class Group:
    def __init__(self):
        self.copies = []

    def add(self, copy, sends, gets):
        self.copies.append((copy, sends, gets))

    def start(self):
        for copy, sends, _ in self.copies:
            pl.when(sends)(copy.start)

    def wait_recv(self):
        for copy, _, gets in self.copies:
            pl.when(gets)(copy.wait_recv)

    def wait_send(self):
        for copy, sends, _ in self.copies:
            pl.when(sends)(copy.wait_send)


def kernel(
    n_sec, n_depth, fields, block_ids, buoyancy, lame_lambda, lame_mu, moments, owners, cells, rows, out,
    tables, staged, staged_ids, state, ids, counts, coefs, raw_stress, leaving, counted, to_right, to_left, from_left, from_right,
    owner_v, cells_v, rows_v, mom_v, bucket, arrived, lhs, rhs,
    local_sem, core_send, core_recv, raw_send, raw_recv, ids_send, ids_recv, count_send, count_recv, all_send, all_recv,
    first_send, first_recv, second_send, second_recv,
):
    sec, depth, seg = lax.axis_index("sec"), lax.axis_index("depth"), lax.axis_index("segment")
    partner = (sec, depth, 1 - seg)

    def load(k, src, dst):
        return pltpu.make_async_copy(src, dst, local_sem.at[k])

    def remote(src, dst, send, recv, to):
        return pltpu.make_async_remote_copy(
            src_ref=src, dst_ref=dst, send_sem=send, recv_sem=recv, device_id=to, device_id_type=MESH
        )

    def there(dx, dz):
        return in_range(sec + dx, depth + dz, n_sec, n_depth)

    loads = [load(0, owners, owner_v), load(1, cells, cells_v), load(2, moments, mom_v), load(3, rows, rows_v)]
    table_loads = [load(10 + k, table, tables.at[k]) for k, table in enumerate((buoyancy, lame_lambda, lame_mu))]
    for copy in loads + table_loads:
        copy.start()

    staged[...] = jnp.zeros_like(staged)
    staged_ids[...] = jnp.full_like(staged_ids, -1)
    state[0, 3:9] = jnp.zeros_like(state[0, 3:9])
    counts[...] = jnp.zeros_like(counts)
    if n_sec < BUCKETS:
        arrived[...] = jnp.zeros_like(arrived)

    barrier = pltpu.get_barrier_semaphore()
    expected = jnp.int32(n_sec)

    @pl.loop(1, n_sec)
    def _(j):
        pl.semaphore_signal(barrier, inc=1, device_id=(lax.rem(sec + j, n_sec), depth, seg), device_id_type=MESH)

    pl.semaphore_signal(barrier, inc=1, device_id=partner, device_id_type=MESH)
    for dx, dz in NEAR:
        if dz != 0:
            near = there(dx, dz)
            expected = expected + near.astype(I32)

            @pl.when(near)
            def _():
                pl.semaphore_signal(barrier, inc=1, device_id=(sec + dx, depth + dz, seg), device_id_type=MESH)

    own_state = load(4, fields.at[0], staged.at[:, OWN_X, rows_at(RIM, CZ)])
    own_ids = load(5, block_ids.at[0], staged_ids.at[OWN_X, rows_at(RIM, CZ)])
    own_stress = load(6, fields.at[0, 3:9], raw_stress)
    own_state.start()
    own_ids.start()
    pl.when(seg == 0)(own_stress.start)

    for copy in loads:
        copy.wait()
    fill_buckets(owner_v, cells_v, mom_v, bucket, lhs, rhs)

    pl.semaphore_wait(barrier, expected)

    offsets = by_distance(n_sec)

    def passed(slot):
        to = lax.rem(sec + offsets[slot - 1], n_sec)
        return remote(
            bucket.at[lax.rem(to, 2) * 16 + to // 2], arrived.at[slot], all_send.at[slot], all_recv.at[slot], (to, depth, seg)
        )

    for slot in reversed(range(1, n_sec)):
        passed(slot).start()

    arrived[0] = bucket[lax.rem(sec, 2) * 16 + sec // 2]

    raw, raw_ids = Group(), Group()
    for q, (dx, dz) in enumerate(NEAR):
        from_z = {-1: rows_at(0, RIM), 0: rows_at(0, CZ), 1: rows_at(CZ - RIM, RIM)}[dz]
        to_z = {-1: rows_at(RIM + CZ, RIM), 0: rows_at(RIM, CZ), 1: rows_at(0, RIM)}[dz]
        to = (sec + dx, depth + dz, seg)
        sends, gets = there(dx, dz), there(-dx, -dz)
        for m, parts in ((0, slice(0, 3)), (1, slice(0, 9))):
            raw.add(
                remote(fields.at[0, parts, :, from_z], staged.at[parts, beside(dx), to_z], raw_send.at[q], raw_recv.at[q], to),
                jnp.logical_and(sends, seg == m), jnp.logical_and(gets, seg == m),
            )
        raw_ids.add(
            remote(block_ids.at[0, :, from_z], staged_ids.at[beside(dx), to_z], ids_send.at[q], ids_recv.at[q], to),
            sends, gets,
        )
    partner_stress = remote(fields.at[0, 3:9], raw_stress, core_send.at[0], core_recv.at[0], partner)
    raw_ids.start()
    pl.when(seg == 0)(partner_stress.start)
    raw.start()

    def window(source, target, send, recv):
        group = Group()
        for c in range(2):
            dz = 1 - 2 * c
            for q, (dx, goes) in enumerate(((-1, 0), (1, 0), (0, dz), (-1, dz), (1, dz))):
                if goes == 0:
                    from_z, to_z = rows_at(RIM * c, HZ + RIM), rows_at(RIM * (1 - c), HZ + RIM)
                else:
                    from_z, to_z = rows_at((CZ - RIM) * (1 - c), RIM), rows_at((HZ + RIM) * c, RIM)
                group.add(
                    remote(source(from_z), target(beside(dx), to_z), send.at[q], recv.at[q], (sec + dx, depth + goes, seg)),
                    jnp.logical_and(there(dx, goes), seg == c), jnp.logical_and(there(-dx, -goes), seg == c),
                )
        return group

    count_rows(rows_v, counted, lhs, rhs)
    for c in range(2):
        @pl.when(seg == c)
        def _():
            counts[OWN_X, rows_at(RIM * (1 - c), HZ + RIM)] = counted[:, rows_at(RIM * c, HZ + RIM)]

    near_counts = window(lambda z: counted.at[:, z], lambda x, z: counts.at[x, z], count_send, count_recv)
    near_counts.start()

    pl.when(seg == 0)(own_stress.wait)
    pl.when(seg == 1)(partner_stress.wait_recv)

    for slot in range(1, min(16, n_sec)):
        passed(slot).wait_recv()
    near_sums = spread_buckets(arrived, 0, lhs, rhs)
    for k in range(6):
        for x in range(CX):
            raw_stress[k, x] += near_sums[k * 16:(k + 1) * 16, x * 128:(x + 1) * 128]
    for slot in range(16, n_sec):
        passed(slot).wait_recv()
    far_sums = spread_buckets(arrived, 1, lhs, rhs)
    for k in range(6):
        for x in range(CX):
            leaving[k, x] = raw_stress[k, x] + far_sums[k * 16:(k + 1) * 16, x * 128:(x + 1) * 128]
    first = window(lambda z: leaving.at[:, :, z], lambda x, z: state.at[0, 3:9, x, z], first_send, first_recv)
    first.start()
    for c in range(2):
        @pl.when(seg == c)
        def _():
            state[0, 3:9, OWN_X, rows_at(RIM * (1 - c), HZ + RIM)] = leaving[:, :, rows_at(RIM * c, HZ + RIM)]

    own_ids.wait()
    raw_ids.wait_recv()
    hand_ids, keep_ids, hand, keep = [], [], [], []
    for m, parts in ((0, slice(0, 3)), (1, slice(0, 9))):
        mine, theirs = rows_at(HZ * m, RZ), rows_at(HZ * (1 - m), RZ)
        hand_ids.append(remote(staged_ids.at[:, theirs], ids.at[m], core_send.at[1], core_recv.at[1], partner))
        keep_ids.append(load(7, staged_ids.at[:, mine], ids.at[m]))
        hand.append(remote(staged.at[parts, :, theirs], state.at[m, parts], core_send.at[2], core_recv.at[2], partner))
        keep.append(load(8, staged.at[parts, :, mine], state.at[m, parts]))

        @pl.when(seg == m)
        def _():
            hand_ids[m].start()
            keep_ids[m].start()

    own_state.wait()
    raw.wait_recv()
    for m in range(2):
        @pl.when(seg == m)
        def _():
            hand[m].start()
            keep[m].start()
    for m in range(2):
        @pl.when(seg == m)
        def _():
            keep_ids[m].wait()
            hand_ids[1 - m].wait_recv()
    for copy in table_loads:
        copy.wait()
    look_up(ids, tables, coefs)
    for m in range(2):
        @pl.when(seg == m)
        def _():
            keep[m].wait()
            hand[1 - m].wait_recv()
    near_counts.wait_recv()
    first.wait_recv()

    lo, hi = X0, X0 + CX - 1
    velocity(state, coefs, counts, range(lo - 1, hi + 3))
    stress(state, coefs, range(lo - 1, hi + 2))
    velocity(state, coefs, counts, range(lo, hi + 2))
    stress(state, coefs, range(lo, hi + 1))
    velocity(state, coefs, counts, (hi,))
    for m in range(2):
        for k in range(3):
            to_right[m, k] = state[m, k, hi]
            to_left[m, k] = state[m, k, hi]
        for k, part in enumerate((3, 7, 8)):
            to_right[m, 3 + k] = state[m, part, hi]
        for k in range(3, 9):
            to_left[m, k] = state[m, k, lo]

    second = Group()
    z = rows_at(2, RZ - 4)
    for q, (dx, src, dst) in enumerate(((1, to_right, from_left), (-1, to_left, from_right))):
        second.add(
            remote(src.at[:, :, z], dst.at[:, :, z], second_send.at[q], second_recv.at[q], (sec + dx, depth, seg)),
            there(dx, 0), there(-dx, 0),
        )
    second.start()
    second.wait_recv()

    @pl.when(there(-1, 0))
    def _():
        for m in range(2):
            for k, part in enumerate((0, 1, 2, 3, 7, 8)):
                state[m, part, lo - 1] = from_left[m, k]

    @pl.when(there(1, 0))
    def _():
        for m in range(2):
            for k in range(3):
                state[m, k, hi + 2] = from_right[m, k]
            for k in range(3, 9):
                state[m, k, hi + 1] = from_right[m, k]

    velocity(state, coefs, counts, (lo, hi + 1))
    stress(state, coefs, range(lo - 1, hi + 2))
    velocity(state, coefs, counts, range(lo, hi + 2))
    stress(state, coefs, range(lo, hi + 1))

    results = []
    for c in range(2):
        part = rows_at(HZ * c, HZ)
        keeps = load(9, state.at[c, :, OWN_X, OWN_Z], out.at[0, :, :, part])
        gives = remote(state.at[1 - c, :, OWN_X, OWN_Z], out.at[0, :, :, part], core_send.at[3], core_recv.at[3], partner)
        results.append((keeps, gives))

        @pl.when(seg == c)
        def _():
            gives.start()
            keeps.start()

    for group in (raw, raw_ids, near_counts, first, second):
        group.wait_send()
    pl.when(seg == 0)(partner_stress.wait_send)
    for c in range(2):
        @pl.when(seg == c)
        def _():
            hand_ids[c].wait_send()
            hand[c].wait_send()

    for slot in range(1, n_sec):
        passed(slot).wait_send()

    for c in range(2):
        @pl.when(seg == c)
        def _():
            results[c][0].wait()
            results[c][1].wait_send()
            results[1 - c][1].wait_recv()


def on_device(
    n_sec, n_depth, fields, block_ids, buoyancy, lame_lambda, lame_mu, moments, moment_owner, moment_cells, drm_rows
):
    owners = moment_owner.reshape(ENT // 128, 128)
    cells = moment_cells.reshape(ENT // 128, 128)
    rows = drm_rows.reshape(ROWS // 128, 128)
    hbm = pl.BlockSpec(memory_space=pl.ANY)
    dma = pltpu.SemaphoreType.DMA
    vmem = pltpu.VMEM
    return pl.pallas_call(
        functools.partial(kernel, n_sec, n_depth),
        out_shape=pltpu.VMEM(fields.shape, F32),
        in_specs=[hbm] * 9,
        out_specs=pl.BlockSpec(memory_space=pltpu.VMEM),
        scratch_shapes=[
            pltpu.SMEM((3, 16), F32),
            vmem((9, PX, GZ, CY), F32),
            vmem((PX, GZ, CY), I32),
            vmem((2, 9, PX, RZ, CY), F32),
            vmem((2, PX, RZ, CY), I32),
            vmem((PX, RZ, CY), F32),
            vmem((2, 3, PX, RZ, CY), F32),
            vmem((6, CX, CZ, CY), F32),
            vmem((6, CX, CZ, CY), F32),
            vmem((CX, CZ, CY), F32),
            vmem((2, 6, RZ, CY), F32),
            vmem((2, 9, RZ, CY), F32),
            vmem((2, 6, RZ, CY), F32),
            vmem((2, 9, RZ, CY), F32),
            vmem((ENT // 128, 128), I32),
            vmem((ENT // 128, 128), I32),
            vmem((ROWS // 128, 128), I32),
            vmem((6, ENT), F32),
            vmem((BUCKETS, 4, 128), F32),
            vmem((BUCKETS, 4, 128), F32),
            vmem((192, 2048), BF16),
            vmem((256, 2048), BF16),
            dma((13,)),
            dma((4,)), dma((4,)),
            dma((8,)), dma((8,)),
            dma((8,)), dma((8,)),
            dma((5,)), dma((5,)),
            dma((BUCKETS,)), dma((BUCKETS,)),
            dma((5,)), dma((5,)),
            dma((2,)), dma((2,)),
        ],
        compiler_params=pltpu.CompilerParams(collective_id=0, has_side_effects=True),
    )(fields, block_ids, buoyancy, lame_lambda, lame_mu, moments, owners, cells, rows)


def solution(mesh):
    in_specs = (
        P("segment", None, "sec", "depth", None),
        P("segment", "sec", "depth", None),
        P(),
        P(),
        P(),
        P(None, ("sec", "depth")),
        P(("sec", "depth"), None),
        P(("sec", "depth")),
        P(("sec", "depth")),
    )
    return jax.shard_map(
        functools.partial(on_device, mesh.shape["sec"], mesh.shape["depth"]),
        mesh=mesh, in_specs=in_specs, out_specs=P("segment", None, "sec", "depth", None), check_vma=False,
    )
```

```python
import functools

import jax
import jax.numpy as jnp
from jax import lax
from jax.experimental import pallas as pl
from jax.experimental.pallas import tpu as pltpu
from jax.sharding import PartitionSpec as P

MESH = pl.DeviceIdType.MESH
CX, CZ, CY = 2, 16, 128
ENT, ROWS, CAP, BUCKETS = 1024, 2048, 64, 32
HZ, RIM = CZ // 2, 4
PX, RZ, GZ = CX + 4, HZ + 2 * RIM, CZ + 2 * RIM
X0 = 2
OWN_X, OWN_Z = slice(X0, X0 + CX), slice(RIM, RIM + HZ)
NEAR = tuple((dx, dz) for dx in (-1, 0, 1) for dz in (-1, 0, 1) if (dx, dz) != (0, 0))
NT = (((1,), (1,)), ((), ()))
BF16, F32, I32 = jnp.bfloat16, jnp.float32, jnp.int32


def split(value):
    high = value.astype(BF16).astype(F32)
    return high, value - high


def rows_at(start, size):
    return slice(start, start + size)


def beside(dx):
    return rows_at(X0 - CX * dx, CX)


def in_range(sec, depth, n_sec, n_depth):
    ok_sec = jnp.logical_and(sec >= 0, sec < n_sec)
    ok_depth = jnp.logical_and(depth >= 0, depth < n_depth)
    return jnp.logical_and(ok_sec, ok_depth)


def fill_buckets(owner, cells, mom, bucket, lhs, rhs):
    owners = [owner[t:t + 1, :] for t in range(8)]
    row32 = lax.broadcasted_iota(I32, (BUCKETS, 128), 0)
    hot = [jnp.where(row32 == o, 1.0, 0.0) for o in owners]
    before = jnp.where(
        lax.broadcasted_iota(I32, (128, 256), 0) < lax.broadcasted_iota(I32, (128, 256), 1), 1.0, 0.0
    ).astype(BF16)
    counts = jnp.dot(jnp.concatenate(hot, 0).astype(BF16), before, preferred_element_type=F32)
    running = jnp.zeros((BUCKETS, 128), F32)
    row16 = lax.broadcasted_iota(I32, (16, 128), 0)
    row256 = lax.broadcasted_iota(I32, (256, 128), 0)
    for t in range(8):
        part = counts[t * BUCKETS:(t + 1) * BUCKETS]
        rank = jnp.sum(hot[t] * (part[:, :128] + running), axis=0, keepdims=True).astype(I32)
        running = running + part[:, 128:]
        cols = slice(t * 128, (t + 1) * 128)
        slot = (owners[t] & 1) * 128 + rank
        mine = row16 == (owners[t] >> 1)
        cell = cells[t:t + 1, :].astype(F32)
        for h in range(2):
            at = slice((2 * t + h) * 128, (2 * t + h + 1) * 128)
            rhs[:, at] = jnp.where(row256 == slot + h * CAP, 1.0, 0.0).astype(BF16)
            for j in range(4):
                value = mom[2 * j + h:2 * j + h + 1, cols] if j < 3 else cell
                high, low = split(value)
                lhs[j * 16:(j + 1) * 16, at] = jnp.where(mine, high, 0.0).astype(BF16)
                lhs[64 + j * 16:64 + (j + 1) * 16, at] = jnp.where(mine, low, 0.0).astype(BF16)
    sums = lax.dot_general(lhs[0:128, :], rhs[...], NT, preferred_element_type=F32)
    sums = sums[0:64] + sums[64:128]
    for j in range(4):
        for x in range(2):
            bucket[x * 16:(x + 1) * 16, j, :] = sums[j * 16:(j + 1) * 16, x * 128:(x + 1) * 128]


def place(cell):
    return (cell >> 7) & 15, ((cell >> 11) << 7) | (cell & 127)


def by_distance(n_sec):
    def hops(offset):
        row, col = offset // 4, offset % 4
        return min(row, n_sec // 4 - row) + min(col, 4 - col)

    return sorted(range(1, n_sec), key=hops)


def spread_buckets(arrived, batch, lhs, rhs):
    low_half = lax.broadcasted_iota(I32, (8, 128), 1) < CAP
    values, cell = [], None
    for j in range(4):
        a, b = arrived[batch * 16:batch * 16 + 8, j, :], arrived[batch * 16 + 8:batch * 16 + 16, j, :]
        even = jnp.where(low_half, a, pltpu.roll(b, CAP, 1))
        if j < 3:
            values.append(even)
            values.append(jnp.where(low_half, pltpu.roll(a, CAP, 1), b))
        else:
            cell = even.astype(I32)
    z, lane = place(cell)
    parts = [split(value) for value in values]
    row16 = lax.broadcasted_iota(I32, (16, 128), 0)
    row256 = lax.broadcasted_iota(I32, (256, 128), 0)
    half = slice(batch * 1024, (batch + 1) * 1024)
    for t in range(8):
        at = slice(batch * 1024 + t * 128, batch * 1024 + (t + 1) * 128)
        mine = row16 == z[t:t + 1]
        rhs[:, at] = jnp.where(row256 == lane[t:t + 1], 1.0, 0.0).astype(BF16)
        for k, (high, low) in enumerate(parts):
            lhs[k * 16:(k + 1) * 16, at] = jnp.where(mine, high[t:t + 1], 0.0).astype(BF16)
            lhs[96 + k * 16:96 + (k + 1) * 16, at] = jnp.where(mine, low[t:t + 1], 0.0).astype(BF16)
    sums = lax.dot_general(lhs[:, half], rhs[:, half], NT, preferred_element_type=F32)
    return sums[0:96] + sums[96:192]


def count_rows(rows, counted, lhs, rhs):
    z, lane = place(rows[...])
    row16 = lax.broadcasted_iota(I32, (16, 128), 0)
    row256 = lax.broadcasted_iota(I32, (256, 128), 0)
    for t in range(16):
        at = slice(t * 128, (t + 1) * 128)
        lhs[0:16, at] = jnp.where(row16 == z[t:t + 1], 1.0, 0.0).astype(BF16)
        rhs[:, at] = jnp.where(row256 == lane[t:t + 1], 1.0, 0.0).astype(BF16)
    sums = lax.dot_general(lhs[0:16, :], rhs[...], NT, preferred_element_type=F32)
    for x in range(CX):
        counted[x] = sums[:, x * 128:(x + 1) * 128]


def place(cell):
    return (cell >> 7) & 15, ((cell >> 11) << 7) | (cell & 127)


def look_up(ids, tables, coefs):
    for m in range(2):
        for p in range(PX):
            block = ids[m, p]
            values = [jnp.zeros((RZ, CY), F32) for _ in range(3)]
            for entry in range(16):
                here = block == entry
                values = [jnp.where(here, tables[k, entry], v) for k, v in enumerate(values)]
            for k, v in enumerate(values):
                coefs[m, k, p] = 0.5 * v


def y_before(f, first):
    return jnp.where(first, 0.0, pltpu.roll(f, 1, 1))


def y_after(f, last):
    return jnp.where(last, 0.0, pltpu.roll(f, CY - 1, 1))


def z_before(f):
    return pltpu.roll(f, 1, 0)


def z_after(f):
    return pltpu.roll(f, RZ - 1, 0)


def increments(state, coefs, m, p):
    first = lax.broadcasted_iota(I32, (RZ, CY), 1) == 0
    b = coefs[m, 0, p]
    sxx, syy, szz, syz, sxz, sxy = (state[m, k, p] for k in range(3, 9))
    bxx, bxz, bxy = (state[m, k, p - 1] for k in (3, 7, 8))
    ix = b * ((sxx - bxx) + (sxy - y_before(sxy, first)) + (sxz - z_before(sxz)))
    iy = b * ((sxy - bxy) + (syy - y_before(syy, first)) + (syz - z_before(syz)))
    iz = b * ((sxz - bxz) + (syz - y_before(syz, first)) + (szz - z_before(szz)))
    return ix, iy, iz


def velocity(state, coefs, counts, planes):
    for p in planes:
        count = counts[p]
        regional, basin = increments(state, coefs, 0, p), increments(state, coefs, 1, p)
        for k in range(3):
            state[0, k, p] += regional[k]
            state[1, k, p] += basin[k] + count * regional[k]


def stress(state, coefs, planes):
    last = lax.broadcasted_iota(I32, (RZ, CY), 1) == CY - 1
    for m in range(2):
        for p in planes:
            lam, mu = coefs[m, 1, p], coefs[m, 2, p]
            vx, vy, vz = (state[m, k, p] for k in range(3))
            ax, ay, az = (state[m, k, p + 1] for k in range(3))
            exx = ax - vx
            eyy = y_after(vy, last) - vy
            ezz = z_after(vz) - vz
            bulk = lam * (exx + eyy + ezz)
            mu2 = mu + mu
            state[m, 3, p] += bulk + mu2 * exx
            state[m, 4, p] += bulk + mu2 * eyy
            state[m, 5, p] += bulk + mu2 * ezz
            state[m, 6, p] += mu * ((z_after(vy) - vy) + (y_after(vz, last) - vz))
            state[m, 7, p] += mu * ((z_after(vx) - vx) + (az - vz))
            state[m, 8, p] += mu * ((y_after(vx, last) - vx) + (ay - vy))


class Group:
    def __init__(self):
        self.copies = []

    def add(self, copy, sends, gets):
        self.copies.append((copy, sends, gets))

    def start(self):
        for copy, sends, _ in self.copies:
            pl.when(sends)(copy.start)

    def wait_recv(self):
        for copy, _, gets in self.copies:
            pl.when(gets)(copy.wait_recv)

    def wait_send(self):
        for copy, sends, _ in self.copies:
            pl.when(sends)(copy.wait_send)


def kernel(
    n_sec, n_depth, fields, block_ids, buoyancy, lame_lambda, lame_mu, moments, owners, cells, rows, out,
    tables, staged, staged_ids, state, ids, counts, coefs, raw_stress, leaving, counted, to_right, to_left, from_left, from_right,
    owner_v, cells_v, rows_v, mom_v, bucket, arrived, lhs, rhs,
    local_sem, core_send, core_recv, raw_send, raw_recv, ids_send, ids_recv, count_send, count_recv, all_send, all_recv,
    first_send, first_recv, second_send, second_recv,
):
    sec, depth, seg = lax.axis_index("sec"), lax.axis_index("depth"), lax.axis_index("segment")
    partner = (sec, depth, 1 - seg)

    def load(k, src, dst):
        return pltpu.make_async_copy(src, dst, local_sem.at[k])

    def remote(src, dst, send, recv, to):
        return pltpu.make_async_remote_copy(
            src_ref=src, dst_ref=dst, send_sem=send, recv_sem=recv, device_id=to, device_id_type=MESH
        )

    def there(dx, dz):
        return in_range(sec + dx, depth + dz, n_sec, n_depth)

    offsets = by_distance(n_sec)
    barrier = pltpu.get_barrier_semaphore()

    def greet(offset):
        to = (lax.rem(sec + offset, n_sec), depth, seg)
        pl.semaphore_signal(barrier, inc=1, device_id=to, device_id_type=MESH)

    for offset in reversed(offsets):
        if offset not in (1, n_sec - 1):
            greet(offset)

    loads = [load(0, owners, owner_v), load(1, cells, cells_v), load(2, moments, mom_v), load(3, rows, rows_v)]
    table_loads = [load(10 + k, table, tables.at[k]) for k, table in enumerate((buoyancy, lame_lambda, lame_mu))]
    for copy in loads + table_loads:
        copy.start()

    staged[...] = jnp.zeros_like(staged)
    staged_ids[...] = jnp.full_like(staged_ids, -1)
    state[0, 3:9] = jnp.zeros_like(state[0, 3:9])
    counts[...] = jnp.zeros_like(counts)
    if n_sec < BUCKETS:
        arrived[...] = jnp.zeros_like(arrived)

    expected = jnp.int32(n_sec)
    greet(1)
    greet(n_sec - 1)
    pl.semaphore_signal(barrier, inc=1, device_id=partner, device_id_type=MESH)
    for dx, dz in NEAR:
        if dz != 0:
            near = there(dx, dz)
            expected = expected + near.astype(I32)

            @pl.when(near)
            def _():
                pl.semaphore_signal(barrier, inc=1, device_id=(sec + dx, depth + dz, seg), device_id_type=MESH)

    own_state = load(4, fields.at[0], staged.at[:, OWN_X, rows_at(RIM, CZ)])
    own_ids = load(5, block_ids.at[0], staged_ids.at[OWN_X, rows_at(RIM, CZ)])
    own_stress = load(6, fields.at[0, 3:9], raw_stress)
    own_state.start()
    own_ids.start()
    pl.when(seg == 0)(own_stress.start)

    for copy in loads:
        copy.wait()
    fill_buckets(owner_v, cells_v, mom_v, bucket, lhs, rhs)

    pl.semaphore_wait(barrier, expected)

    def passed(slot):
        to = lax.rem(sec + offsets[slot - 1], n_sec)
        return remote(
            bucket.at[lax.rem(to, 2) * 16 + to // 2], arrived.at[slot], all_send.at[slot], all_recv.at[slot], (to, depth, seg)
        )

    for slot in reversed(range(1, n_sec)):
        passed(slot).start()

    arrived[0] = bucket[lax.rem(sec, 2) * 16 + sec // 2]

    raw, raw_ids = Group(), Group()
    for q, (dx, dz) in enumerate(NEAR):
        from_z = {-1: rows_at(0, RIM), 0: rows_at(0, CZ), 1: rows_at(CZ - RIM, RIM)}[dz]
        to_z = {-1: rows_at(RIM + CZ, RIM), 0: rows_at(RIM, CZ), 1: rows_at(0, RIM)}[dz]
        to = (sec + dx, depth + dz, seg)
        sends, gets = there(dx, dz), there(-dx, -dz)
        for m, parts in ((0, slice(0, 3)), (1, slice(0, 9))):
            raw.add(
                remote(fields.at[0, parts, :, from_z], staged.at[parts, beside(dx), to_z], raw_send.at[q], raw_recv.at[q], to),
                jnp.logical_and(sends, seg == m), jnp.logical_and(gets, seg == m),
            )
        raw_ids.add(
            remote(block_ids.at[0, :, from_z], staged_ids.at[beside(dx), to_z], ids_send.at[q], ids_recv.at[q], to),
            sends, gets,
        )
    partner_stress = remote(fields.at[0, 3:9], raw_stress, core_send.at[0], core_recv.at[0], partner)
    raw_ids.start()
    pl.when(seg == 0)(partner_stress.start)
    raw.start()

    def window(source, target, send, recv):
        group = Group()
        for c in range(2):
            dz = 1 - 2 * c
            for q, (dx, goes) in enumerate(((-1, 0), (1, 0), (0, dz), (-1, dz), (1, dz))):
                if goes == 0:
                    from_z, to_z = rows_at(RIM * c, HZ + RIM), rows_at(RIM * (1 - c), HZ + RIM)
                else:
                    from_z, to_z = rows_at((CZ - RIM) * (1 - c), RIM), rows_at((HZ + RIM) * c, RIM)
                group.add(
                    remote(source(from_z), target(beside(dx), to_z), send.at[q], recv.at[q], (sec + dx, depth + goes, seg)),
                    jnp.logical_and(there(dx, goes), seg == c), jnp.logical_and(there(-dx, -goes), seg == c),
                )
        return group

    count_rows(rows_v, counted, lhs, rhs)
    for c in range(2):
        @pl.when(seg == c)
        def _():
            counts[OWN_X, rows_at(RIM * (1 - c), HZ + RIM)] = counted[:, rows_at(RIM * c, HZ + RIM)]

    near_counts = window(lambda z: counted.at[:, z], lambda x, z: counts.at[x, z], count_send, count_recv)
    near_counts.start()

    pl.when(seg == 0)(own_stress.wait)
    pl.when(seg == 1)(partner_stress.wait_recv)

    for slot in range(1, min(16, n_sec)):
        passed(slot).wait_recv()
    near_sums = spread_buckets(arrived, 0, lhs, rhs)
    for k in range(6):
        for x in range(CX):
            raw_stress[k, x] += near_sums[k * 16:(k + 1) * 16, x * 128:(x + 1) * 128]
    for slot in range(16, n_sec):
        passed(slot).wait_recv()
    far_sums = spread_buckets(arrived, 1, lhs, rhs)
    for k in range(6):
        for x in range(CX):
            leaving[k, x] = raw_stress[k, x] + far_sums[k * 16:(k + 1) * 16, x * 128:(x + 1) * 128]
    first = window(lambda z: leaving.at[:, :, z], lambda x, z: state.at[0, 3:9, x, z], first_send, first_recv)
    first.start()
    for c in range(2):
        @pl.when(seg == c)
        def _():
            state[0, 3:9, OWN_X, rows_at(RIM * (1 - c), HZ + RIM)] = leaving[:, :, rows_at(RIM * c, HZ + RIM)]

    own_ids.wait()
    raw_ids.wait_recv()
    hand_ids, keep_ids, hand, keep = [], [], [], []
    for m, parts in ((0, slice(0, 3)), (1, slice(0, 9))):
        mine, theirs = rows_at(HZ * m, RZ), rows_at(HZ * (1 - m), RZ)
        hand_ids.append(remote(staged_ids.at[:, theirs], ids.at[m], core_send.at[1], core_recv.at[1], partner))
        keep_ids.append(load(7, staged_ids.at[:, mine], ids.at[m]))
        hand.append(remote(staged.at[parts, :, theirs], state.at[m, parts], core_send.at[2], core_recv.at[2], partner))
        keep.append(load(8, staged.at[parts, :, mine], state.at[m, parts]))

        @pl.when(seg == m)
        def _():
            hand_ids[m].start()
            keep_ids[m].start()

    own_state.wait()
    raw.wait_recv()
    for m in range(2):
        @pl.when(seg == m)
        def _():
            hand[m].start()
            keep[m].start()
    for m in range(2):
        @pl.when(seg == m)
        def _():
            keep_ids[m].wait()
            hand_ids[1 - m].wait_recv()
    for copy in table_loads:
        copy.wait()
    look_up(ids, tables, coefs)
    for m in range(2):
        @pl.when(seg == m)
        def _():
            keep[m].wait()
            hand[1 - m].wait_recv()
    near_counts.wait_recv()
    first.wait_recv()

    lo, hi = X0, X0 + CX - 1
    velocity(state, coefs, counts, range(lo - 1, hi + 3))
    stress(state, coefs, range(lo - 1, hi + 2))
    velocity(state, coefs, counts, range(lo, hi + 2))
    stress(state, coefs, range(lo, hi + 1))
    velocity(state, coefs, counts, (hi,))
    for m in range(2):
        for k in range(3):
            to_right[m, k] = state[m, k, hi]
            to_left[m, k] = state[m, k, hi]
        for k, part in enumerate((3, 7, 8)):
            to_right[m, 3 + k] = state[m, part, hi]
        for k in range(3, 9):
            to_left[m, k] = state[m, k, lo]

    second = Group()
    z = rows_at(2, RZ - 4)
    for q, (dx, src, dst) in enumerate(((1, to_right, from_left), (-1, to_left, from_right))):
        second.add(
            remote(src.at[:, :, z], dst.at[:, :, z], second_send.at[q], second_recv.at[q], (sec + dx, depth, seg)),
            there(dx, 0), there(-dx, 0),
        )
    second.start()
    second.wait_recv()

    @pl.when(there(-1, 0))
    def _():
        for m in range(2):
            for k, part in enumerate((0, 1, 2, 3, 7, 8)):
                state[m, part, lo - 1] = from_left[m, k]

    @pl.when(there(1, 0))
    def _():
        for m in range(2):
            for k in range(3):
                state[m, k, hi + 2] = from_right[m, k]
            for k in range(3, 9):
                state[m, k, hi + 1] = from_right[m, k]

    velocity(state, coefs, counts, (lo, hi + 1))
    stress(state, coefs, range(lo - 1, hi + 2))
    velocity(state, coefs, counts, range(lo, hi + 2))
    stress(state, coefs, range(lo, hi + 1))

    results = []
    for c in range(2):
        part = rows_at(HZ * c, HZ)
        keeps = load(9, state.at[c, :, OWN_X, OWN_Z], out.at[0, :, :, part])
        gives = remote(state.at[1 - c, :, OWN_X, OWN_Z], out.at[0, :, :, part], core_send.at[3], core_recv.at[3], partner)
        results.append((keeps, gives))

        @pl.when(seg == c)
        def _():
            gives.start()
            keeps.start()

    for group in (raw, raw_ids, near_counts, first, second):
        group.wait_send()
    pl.when(seg == 0)(partner_stress.wait_send)
    for c in range(2):
        @pl.when(seg == c)
        def _():
            hand_ids[c].wait_send()
            hand[c].wait_send()

    for slot in range(1, n_sec):
        passed(slot).wait_send()

    for c in range(2):
        @pl.when(seg == c)
        def _():
            results[c][0].wait()
            results[c][1].wait_send()
            results[1 - c][1].wait_recv()


def on_device(
    n_sec, n_depth, fields, block_ids, buoyancy, lame_lambda, lame_mu, moments, moment_owner, moment_cells, drm_rows
):
    owners = moment_owner.reshape(ENT // 128, 128)
    cells = moment_cells.reshape(ENT // 128, 128)
    rows = drm_rows.reshape(ROWS // 128, 128)
    hbm = pl.BlockSpec(memory_space=pl.ANY)
    dma = pltpu.SemaphoreType.DMA
    vmem = pltpu.VMEM
    return pl.pallas_call(
        functools.partial(kernel, n_sec, n_depth),
        out_shape=pltpu.VMEM(fields.shape, F32),
        in_specs=[hbm] * 9,
        out_specs=pl.BlockSpec(memory_space=pltpu.VMEM),
        scratch_shapes=[
            pltpu.SMEM((3, 16), F32),
            vmem((9, PX, GZ, CY), F32),
            vmem((PX, GZ, CY), I32),
            vmem((2, 9, PX, RZ, CY), F32),
            vmem((2, PX, RZ, CY), I32),
            vmem((PX, RZ, CY), F32),
            vmem((2, 3, PX, RZ, CY), F32),
            vmem((6, CX, CZ, CY), F32),
            vmem((6, CX, CZ, CY), F32),
            vmem((CX, CZ, CY), F32),
            vmem((2, 6, RZ, CY), F32),
            vmem((2, 9, RZ, CY), F32),
            vmem((2, 6, RZ, CY), F32),
            vmem((2, 9, RZ, CY), F32),
            vmem((ENT // 128, 128), I32),
            vmem((ENT // 128, 128), I32),
            vmem((ROWS // 128, 128), I32),
            vmem((6, ENT), F32),
            vmem((BUCKETS, 4, 128), F32),
            vmem((BUCKETS, 4, 128), F32),
            vmem((192, 2048), BF16),
            vmem((256, 2048), BF16),
            dma((13,)),
            dma((4,)), dma((4,)),
            dma((8,)), dma((8,)),
            dma((8,)), dma((8,)),
            dma((5,)), dma((5,)),
            dma((BUCKETS,)), dma((BUCKETS,)),
            dma((5,)), dma((5,)),
            dma((2,)), dma((2,)),
        ],
        compiler_params=pltpu.CompilerParams(collective_id=0, has_side_effects=True),
    )(fields, block_ids, buoyancy, lame_lambda, lame_mu, moments, owners, cells, rows)


def solution(mesh):
    in_specs = (
        P("segment", None, "sec", "depth", None),
        P("segment", "sec", "depth", None),
        P(),
        P(),
        P(),
        P(None, ("sec", "depth")),
        P(("sec", "depth"), None),
        P(("sec", "depth")),
        P(("sec", "depth")),
    )
    return jax.shard_map(
        functools.partial(on_device, mesh.shape["sec"], mesh.shape["depth"]),
        mesh=mesh, in_specs=in_specs, out_specs=P("segment", None, "sec", "depth", None), check_vma=False,
    )
```

```python
import functools

import jax
import jax.numpy as jnp
from jax import lax
from jax.experimental import pallas as pl
from jax.experimental.pallas import tpu as pltpu
from jax.sharding import PartitionSpec as P

MESH = pl.DeviceIdType.MESH
CX, CZ, CY = 2, 16, 128
ENT, ROWS, CAP, BUCKETS = 1024, 2048, 64, 32
HZ, RIM = CZ // 2, 4
PX, RZ, GZ = CX + 4, HZ + 2 * RIM, CZ + 2 * RIM
X0 = 2
OWN_X, OWN_Z = slice(X0, X0 + CX), slice(RIM, RIM + HZ)
NEAR = tuple((dx, dz) for dx in (-1, 0, 1) for dz in (-1, 0, 1) if (dx, dz) != (0, 0))
NT = (((1,), (1,)), ((), ()))
BF16, F32, I32 = jnp.bfloat16, jnp.float32, jnp.int32


def split(value):
    high = value.astype(BF16).astype(F32)
    return high, value - high


def rows_at(start, size):
    return slice(start, start + size)


def beside(dx):
    return rows_at(X0 - CX * dx, CX)


def in_range(sec, depth, n_sec, n_depth):
    ok_sec = jnp.logical_and(sec >= 0, sec < n_sec)
    ok_depth = jnp.logical_and(depth >= 0, depth < n_depth)
    return jnp.logical_and(ok_sec, ok_depth)


def fill_buckets(owner, cells, mom, bucket, lhs, rhs):
    owners = [owner[t:t + 1, :] for t in range(8)]
    row32 = lax.broadcasted_iota(I32, (BUCKETS, 128), 0)
    hot = [jnp.where(row32 == o, 1.0, 0.0) for o in owners]
    before = jnp.where(
        lax.broadcasted_iota(I32, (128, 256), 0) < lax.broadcasted_iota(I32, (128, 256), 1), 1.0, 0.0
    ).astype(BF16)
    counts = jnp.dot(jnp.concatenate(hot, 0).astype(BF16), before, preferred_element_type=F32)
    running = jnp.zeros((BUCKETS, 128), F32)
    row16 = lax.broadcasted_iota(I32, (16, 128), 0)
    row256 = lax.broadcasted_iota(I32, (256, 128), 0)
    for t in range(8):
        part = counts[t * BUCKETS:(t + 1) * BUCKETS]
        rank = jnp.sum(hot[t] * (part[:, :128] + running), axis=0, keepdims=True).astype(I32)
        running = running + part[:, 128:]
        cols = slice(t * 128, (t + 1) * 128)
        slot = (owners[t] & 1) * 128 + rank
        mine = row16 == (owners[t] >> 1)
        cell = cells[t:t + 1, :].astype(F32)
        for h in range(2):
            at = slice((2 * t + h) * 128, (2 * t + h + 1) * 128)
            rhs[:, at] = jnp.where(row256 == slot + h * CAP, 1.0, 0.0).astype(BF16)
            for j in range(4):
                value = mom[2 * j + h:2 * j + h + 1, cols] if j < 3 else cell
                high, low = split(value)
                lhs[j * 16:(j + 1) * 16, at] = jnp.where(mine, high, 0.0).astype(BF16)
                lhs[64 + j * 16:64 + (j + 1) * 16, at] = jnp.where(mine, low, 0.0).astype(BF16)
    sums = lax.dot_general(lhs[0:128, :], rhs[...], NT, preferred_element_type=F32)
    sums = sums[0:64] + sums[64:128]
    for j in range(4):
        for x in range(2):
            bucket[x * 16:(x + 1) * 16, j, :] = sums[j * 16:(j + 1) * 16, x * 128:(x + 1) * 128]


def place(cell):
    return (cell >> 7) & 15, ((cell >> 11) << 7) | (cell & 127)


def by_distance(n_sec):
    def hops(offset):
        row, col = offset // 4, offset % 4
        return min(row, n_sec // 4 - row) + min(col, 4 - col)

    return sorted(range(1, n_sec), key=hops)


def spread_buckets(arrived, batch, lhs, rhs):
    low_half = lax.broadcasted_iota(I32, (8, 128), 1) < CAP
    values, cell = [], None
    for j in range(4):
        a, b = arrived[batch * 16:batch * 16 + 8, j, :], arrived[batch * 16 + 8:batch * 16 + 16, j, :]
        even = jnp.where(low_half, a, pltpu.roll(b, CAP, 1))
        if j < 3:
            values.append(even)
            values.append(jnp.where(low_half, pltpu.roll(a, CAP, 1), b))
        else:
            cell = even.astype(I32)
    z, lane = place(cell)
    parts = [split(value) for value in values]
    row16 = lax.broadcasted_iota(I32, (16, 128), 0)
    row256 = lax.broadcasted_iota(I32, (256, 128), 0)
    half = slice(batch * 1024, (batch + 1) * 1024)
    for t in range(8):
        at = slice(batch * 1024 + t * 128, batch * 1024 + (t + 1) * 128)
        mine = row16 == z[t:t + 1]
        rhs[:, at] = jnp.where(row256 == lane[t:t + 1], 1.0, 0.0).astype(BF16)
        for k, (high, low) in enumerate(parts):
            lhs[k * 16:(k + 1) * 16, at] = jnp.where(mine, high[t:t + 1], 0.0).astype(BF16)
            lhs[96 + k * 16:96 + (k + 1) * 16, at] = jnp.where(mine, low[t:t + 1], 0.0).astype(BF16)
    sums = lax.dot_general(lhs[:, half], rhs[:, half], NT, preferred_element_type=F32)
    return sums[0:96] + sums[96:192]


def count_rows(rows, counted, lhs, rhs):
    z, lane = place(rows[...])
    row16 = lax.broadcasted_iota(I32, (16, 128), 0)
    row256 = lax.broadcasted_iota(I32, (256, 128), 0)
    for t in range(16):
        at = slice(t * 128, (t + 1) * 128)
        lhs[0:16, at] = jnp.where(row16 == z[t:t + 1], 1.0, 0.0).astype(BF16)
        rhs[:, at] = jnp.where(row256 == lane[t:t + 1], 1.0, 0.0).astype(BF16)
    sums = lax.dot_general(lhs[0:16, :], rhs[...], NT, preferred_element_type=F32)
    for x in range(CX):
        counted[x] = sums[:, x * 128:(x + 1) * 128]


def place(cell):
    return (cell >> 7) & 15, ((cell >> 11) << 7) | (cell & 127)


def look_up(ids, tables, coefs):
    for m in range(2):
        for p in range(PX):
            block = ids[m, p]
            values = [jnp.zeros((RZ, CY), F32) for _ in range(3)]
            for entry in range(16):
                here = block == entry
                values = [jnp.where(here, tables[k, entry], v) for k, v in enumerate(values)]
            for k, v in enumerate(values):
                coefs[m, k, p] = 0.5 * v


def y_before(f, first):
    return jnp.where(first, 0.0, pltpu.roll(f, 1, 1))


def y_after(f, last):
    return jnp.where(last, 0.0, pltpu.roll(f, CY - 1, 1))


def z_before(f):
    return pltpu.roll(f, 1, 0)


def z_after(f):
    return pltpu.roll(f, RZ - 1, 0)


def increments(state, coefs, m, p):
    first = lax.broadcasted_iota(I32, (RZ, CY), 1) == 0
    b = coefs[m, 0, p]
    sxx, syy, szz, syz, sxz, sxy = (state[m, k, p] for k in range(3, 9))
    bxx, bxz, bxy = (state[m, k, p - 1] for k in (3, 7, 8))
    ix = b * ((sxx - bxx) + (sxy - y_before(sxy, first)) + (sxz - z_before(sxz)))
    iy = b * ((sxy - bxy) + (syy - y_before(syy, first)) + (syz - z_before(syz)))
    iz = b * ((sxz - bxz) + (syz - y_before(syz, first)) + (szz - z_before(szz)))
    return ix, iy, iz


def velocity(state, coefs, counts, planes):
    for p in planes:
        count = counts[p]
        regional, basin = increments(state, coefs, 0, p), increments(state, coefs, 1, p)
        for k in range(3):
            state[0, k, p] += regional[k]
            state[1, k, p] += basin[k] + count * regional[k]


def stress(state, coefs, planes):
    last = lax.broadcasted_iota(I32, (RZ, CY), 1) == CY - 1
    for m in range(2):
        for p in planes:
            lam, mu = coefs[m, 1, p], coefs[m, 2, p]
            vx, vy, vz = (state[m, k, p] for k in range(3))
            ax, ay, az = (state[m, k, p + 1] for k in range(3))
            exx = ax - vx
            eyy = y_after(vy, last) - vy
            ezz = z_after(vz) - vz
            bulk = lam * (exx + eyy + ezz)
            mu2 = mu + mu
            state[m, 3, p] += bulk + mu2 * exx
            state[m, 4, p] += bulk + mu2 * eyy
            state[m, 5, p] += bulk + mu2 * ezz
            state[m, 6, p] += mu * ((z_after(vy) - vy) + (y_after(vz, last) - vz))
            state[m, 7, p] += mu * ((z_after(vx) - vx) + (az - vz))
            state[m, 8, p] += mu * ((y_after(vx, last) - vx) + (ay - vy))


class Group:
    def __init__(self):
        self.copies = []

    def add(self, copy, sends, gets):
        self.copies.append((copy, sends, gets))

    def start(self):
        for copy, sends, _ in self.copies:
            pl.when(sends)(copy.start)

    def wait_recv(self):
        for copy, _, gets in self.copies:
            pl.when(gets)(copy.wait_recv)

    def wait_send(self):
        for copy, sends, _ in self.copies:
            pl.when(sends)(copy.wait_send)


def kernel(
    n_sec, n_depth, fields, block_ids, buoyancy, lame_lambda, lame_mu, moments, owners, cells, rows, out,
    tables, staged, staged_ids, state, ids, counts, coefs, raw_stress, leaving, counted, to_right, to_left, from_left, from_right,
    owner_v, cells_v, rows_v, mom_v, bucket, arrived, lhs, rhs,
    local_sem, core_send, core_recv, raw_send, raw_recv, ids_send, ids_recv, count_send, count_recv, all_send, all_recv,
    first_send, first_recv, second_send, second_recv,
):
    sec, depth, seg = lax.axis_index("sec"), lax.axis_index("depth"), lax.axis_index("segment")
    partner = (sec, depth, 1 - seg)

    def load(k, src, dst):
        return pltpu.make_async_copy(src, dst, local_sem.at[k])

    def remote(src, dst, send, recv, to):
        return pltpu.make_async_remote_copy(
            src_ref=src, dst_ref=dst, send_sem=send, recv_sem=recv, device_id=to, device_id_type=MESH
        )

    def there(dx, dz):
        return in_range(sec + dx, depth + dz, n_sec, n_depth)

    offsets = by_distance(n_sec)
    barrier = pltpu.get_barrier_semaphore()

    def greet(offset):
        to = (lax.rem(sec + offset, n_sec), depth, seg)
        pl.semaphore_signal(barrier, inc=1, device_id=to, device_id_type=MESH)

    for offset in reversed(offsets):
        if offset not in (1, n_sec - 1):
            greet(offset)

    loads = [load(0, owners, owner_v), load(1, cells, cells_v), load(2, moments, mom_v), load(3, rows, rows_v)]
    table_loads = [load(10 + k, table, tables.at[k]) for k, table in enumerate((buoyancy, lame_lambda, lame_mu))]
    for copy in loads + table_loads:
        copy.start()

    staged[...] = jnp.zeros_like(staged)
    staged_ids[...] = jnp.full_like(staged_ids, -1)
    state[0, 3:9] = jnp.zeros_like(state[0, 3:9])
    counts[...] = jnp.zeros_like(counts)
    if n_sec < BUCKETS:
        arrived[...] = jnp.zeros_like(arrived)

    expected = jnp.int32(n_sec)
    greet(1)
    greet(n_sec - 1)
    pl.semaphore_signal(barrier, inc=1, device_id=partner, device_id_type=MESH)
    for dx, dz in NEAR:
        if dz != 0:
            near = there(dx, dz)
            expected = expected + near.astype(I32)

            @pl.when(near)
            def _():
                pl.semaphore_signal(barrier, inc=1, device_id=(sec + dx, depth + dz, seg), device_id_type=MESH)

    own_state = load(4, fields.at[0], staged.at[:, OWN_X, rows_at(RIM, CZ)])
    own_ids = load(5, block_ids.at[0], staged_ids.at[OWN_X, rows_at(RIM, CZ)])
    own_stress = load(6, fields.at[0, 3:9], raw_stress)
    own_state.start()
    own_ids.start()
    pl.when(seg == 0)(own_stress.start)

    for copy in loads:
        copy.wait()
    fill_buckets(owner_v, cells_v, mom_v, bucket, lhs, rhs)

    pl.semaphore_wait(barrier, expected)

    def passed(slot):
        to = lax.rem(sec + offsets[slot - 1], n_sec)
        return remote(
            bucket.at[lax.rem(to, 2) * 16 + to // 2], arrived.at[slot], all_send.at[slot], all_recv.at[slot], (to, depth, seg)
        )

    for slot in reversed(range(1, n_sec)):
        passed(slot).start()

    arrived[0] = bucket[lax.rem(sec, 2) * 16 + sec // 2]

    raw, raw_ids = Group(), Group()
    for q, (dx, dz) in enumerate(NEAR):
        from_z = {-1: rows_at(0, RIM), 0: rows_at(0, CZ), 1: rows_at(CZ - RIM, RIM)}[dz]
        to_z = {-1: rows_at(RIM + CZ, RIM), 0: rows_at(RIM, CZ), 1: rows_at(0, RIM)}[dz]
        to = (sec + dx, depth + dz, seg)
        sends, gets = there(dx, dz), there(-dx, -dz)
        for m, parts in ((0, slice(0, 3)), (1, slice(0, 9))):
            raw.add(
                remote(fields.at[0, parts, :, from_z], staged.at[parts, beside(dx), to_z], raw_send.at[q], raw_recv.at[q], to),
                jnp.logical_and(sends, seg == m), jnp.logical_and(gets, seg == m),
            )
        raw_ids.add(
            remote(block_ids.at[0, :, from_z], staged_ids.at[beside(dx), to_z], ids_send.at[q], ids_recv.at[q], to),
            sends, gets,
        )
    partner_stress = remote(fields.at[0, 3:9], raw_stress, core_send.at[0], core_recv.at[0], partner)
    raw_ids.start()
    pl.when(seg == 0)(partner_stress.start)
    raw.start()

    def window(source, target, send, recv, trim=False):
        group = Group()
        for c in range(2):
            dz = 1 - 2 * c
            for q, (dx, goes) in enumerate(((-1, 0), (1, 0), (0, dz), (-1, dz), (1, dz))):
                less = 1 if trim and dx == -1 and c == (0 if goes == 0 else 1) else 0
                if goes == 0:
                    from_z, to_z = rows_at(RIM * c, HZ + RIM - less), rows_at(RIM * (1 - c), HZ + RIM - less)
                else:
                    from_z, to_z = rows_at((CZ - RIM) * (1 - c), RIM - less), rows_at((HZ + RIM) * c, RIM - less)
                group.add(
                    remote(source(from_z), target(beside(dx), to_z), send.at[q], recv.at[q], (sec + dx, depth + goes, seg)),
                    jnp.logical_and(there(dx, goes), seg == c), jnp.logical_and(there(-dx, -goes), seg == c),
                )
        return group

    count_rows(rows_v, counted, lhs, rhs)
    for c in range(2):
        @pl.when(seg == c)
        def _():
            counts[OWN_X, rows_at(RIM * (1 - c), HZ + RIM)] = counted[:, rows_at(RIM * c, HZ + RIM)]

    near_counts = window(lambda z: counted.at[:, z], lambda x, z: counts.at[x, z], count_send, count_recv)
    near_counts.start()

    pl.when(seg == 0)(own_stress.wait)
    pl.when(seg == 1)(partner_stress.wait_recv)

    for slot in range(1, min(16, n_sec)):
        passed(slot).wait_recv()
    near_sums = spread_buckets(arrived, 0, lhs, rhs)
    for k in range(6):
        for x in range(CX):
            raw_stress[k, x] += near_sums[k * 16:(k + 1) * 16, x * 128:(x + 1) * 128]
    for slot in range(16, n_sec):
        passed(slot).wait_recv()
    far_sums = spread_buckets(arrived, 1, lhs, rhs)
    for k in range(6):
        for x in range(CX):
            leaving[k, x] = raw_stress[k, x] + far_sums[k * 16:(k + 1) * 16, x * 128:(x + 1) * 128]
    first = window(lambda z: leaving.at[:, :, z], lambda x, z: state.at[0, 3:9, x, z], first_send, first_recv, True)
    first.start()
    for c in range(2):
        @pl.when(seg == c)
        def _():
            state[0, 3:9, OWN_X, rows_at(RIM * (1 - c), HZ + RIM)] = leaving[:, :, rows_at(RIM * c, HZ + RIM)]

    own_ids.wait()
    raw_ids.wait_recv()
    hand_ids, keep_ids, hand, keep = [], [], [], []
    for m, parts in ((0, slice(0, 3)), (1, slice(0, 9))):
        mine, theirs = rows_at(HZ * m, RZ), rows_at(HZ * (1 - m), RZ)
        hand_ids.append(remote(staged_ids.at[:, theirs], ids.at[m], core_send.at[1], core_recv.at[1], partner))
        keep_ids.append(load(7, staged_ids.at[:, mine], ids.at[m]))
        hand.append(remote(staged.at[parts, :, theirs], state.at[m, parts], core_send.at[2], core_recv.at[2], partner))
        keep.append(load(8, staged.at[parts, :, mine], state.at[m, parts]))

        @pl.when(seg == m)
        def _():
            hand_ids[m].start()
            keep_ids[m].start()

    own_state.wait()
    raw.wait_recv()
    for m in range(2):
        @pl.when(seg == m)
        def _():
            hand[m].start()
            keep[m].start()
    for m in range(2):
        @pl.when(seg == m)
        def _():
            keep_ids[m].wait()
            hand_ids[1 - m].wait_recv()
    for copy in table_loads:
        copy.wait()
    look_up(ids, tables, coefs)
    for m in range(2):
        @pl.when(seg == m)
        def _():
            keep[m].wait()
            hand[1 - m].wait_recv()
    near_counts.wait_recv()
    first.wait_recv()

    lo, hi = X0, X0 + CX - 1
    velocity(state, coefs, counts, range(lo - 1, hi + 3))
    stress(state, coefs, range(lo - 1, hi + 2))
    velocity(state, coefs, counts, range(lo, hi + 2))
    stress(state, coefs, range(lo, hi + 1))
    velocity(state, coefs, counts, (hi,))
    for m in range(2):
        for k in range(3):
            to_right[m, k] = state[m, k, hi]
            to_left[m, k] = state[m, k, hi]
        for k, part in enumerate((3, 7, 8)):
            to_right[m, 3 + k] = state[m, part, hi]
        for k in range(3, 9):
            to_left[m, k] = state[m, k, lo]

    second = Group()
    sent = (
        (1, to_right, from_left, rows_at(0, 6), rows_at(RIM - 1, HZ + 3)),
        (-1, to_left, from_right, rows_at(3, 6), rows_at(RIM - 2, HZ + 3)),
        (-1, to_left, from_right, rows_at(0, 3), rows_at(RIM - 1, HZ + 1)),
    )
    for q, (dx, src, dst, kinds, z) in enumerate(sent):
        second.add(
            remote(src.at[:, kinds, z], dst.at[:, kinds, z], second_send.at[q], second_recv.at[q], (sec + dx, depth, seg)),
            there(dx, 0), there(-dx, 0),
        )
    second.start()
    second.wait_recv()

    @pl.when(there(-1, 0))
    def _():
        z = sent[0][4]
        for m in range(2):
            for k, part in enumerate((0, 1, 2, 3, 7, 8)):
                state[m, part, lo - 1, z] = from_left[m, k, z]

    @pl.when(there(1, 0))
    def _():
        for m in range(2):
            for k in range(9):
                z = sent[2][4] if k < 3 else sent[1][4]
                state[m, k, hi + 2 if k < 3 else hi + 1, z] = from_right[m, k, z]

    velocity(state, coefs, counts, (lo, hi + 1))
    stress(state, coefs, range(lo - 1, hi + 2))
    velocity(state, coefs, counts, range(lo, hi + 2))
    stress(state, coefs, range(lo, hi + 1))

    results = []
    for c in range(2):
        part = rows_at(HZ * c, HZ)
        keeps = load(9, state.at[c, :, OWN_X, OWN_Z], out.at[0, :, :, part])
        gives = remote(state.at[1 - c, :, OWN_X, OWN_Z], out.at[0, :, :, part], core_send.at[3], core_recv.at[3], partner)
        results.append((keeps, gives))

        @pl.when(seg == c)
        def _():
            gives.start()
            keeps.start()

    for group in (raw, raw_ids, near_counts, first, second):
        group.wait_send()
    pl.when(seg == 0)(partner_stress.wait_send)
    for c in range(2):
        @pl.when(seg == c)
        def _():
            hand_ids[c].wait_send()
            hand[c].wait_send()

    for slot in range(1, n_sec):
        passed(slot).wait_send()

    for c in range(2):
        @pl.when(seg == c)
        def _():
            results[c][0].wait()
            results[c][1].wait_send()
            results[1 - c][1].wait_recv()


def on_device(
    n_sec, n_depth, fields, block_ids, buoyancy, lame_lambda, lame_mu, moments, moment_owner, moment_cells, drm_rows
):
    owners = moment_owner.reshape(ENT // 128, 128)
    cells = moment_cells.reshape(ENT // 128, 128)
    rows = drm_rows.reshape(ROWS // 128, 128)
    hbm = pl.BlockSpec(memory_space=pl.ANY)
    dma = pltpu.SemaphoreType.DMA
    vmem = pltpu.VMEM
    return pl.pallas_call(
        functools.partial(kernel, n_sec, n_depth),
        out_shape=pltpu.VMEM(fields.shape, F32),
        in_specs=[hbm] * 9,
        out_specs=pl.BlockSpec(memory_space=pltpu.VMEM),
        scratch_shapes=[
            pltpu.SMEM((3, 16), F32),
            vmem((9, PX, GZ, CY), F32),
            vmem((PX, GZ, CY), I32),
            vmem((2, 9, PX, RZ, CY), F32),
            vmem((2, PX, RZ, CY), I32),
            vmem((PX, RZ, CY), F32),
            vmem((2, 3, PX, RZ, CY), F32),
            vmem((6, CX, CZ, CY), F32),
            vmem((6, CX, CZ, CY), F32),
            vmem((CX, CZ, CY), F32),
            vmem((2, 6, RZ, CY), F32),
            vmem((2, 9, RZ, CY), F32),
            vmem((2, 6, RZ, CY), F32),
            vmem((2, 9, RZ, CY), F32),
            vmem((ENT // 128, 128), I32),
            vmem((ENT // 128, 128), I32),
            vmem((ROWS // 128, 128), I32),
            vmem((6, ENT), F32),
            vmem((BUCKETS, 4, 128), F32),
            vmem((BUCKETS, 4, 128), F32),
            vmem((192, 2048), BF16),
            vmem((256, 2048), BF16),
            dma((13,)),
            dma((4,)), dma((4,)),
            dma((8,)), dma((8,)),
            dma((8,)), dma((8,)),
            dma((5,)), dma((5,)),
            dma((BUCKETS,)), dma((BUCKETS,)),
            dma((5,)), dma((5,)),
            dma((3,)), dma((3,)),
        ],
        compiler_params=pltpu.CompilerParams(collective_id=0, has_side_effects=True),
    )(fields, block_ids, buoyancy, lame_lambda, lame_mu, moments, owners, cells, rows)


def solution(mesh):
    in_specs = (
        P("segment", None, "sec", "depth", None),
        P("segment", "sec", "depth", None),
        P(),
        P(),
        P(),
        P(None, ("sec", "depth")),
        P(("sec", "depth"), None),
        P(("sec", "depth")),
        P(("sec", "depth")),
    )
    return jax.shard_map(
        functools.partial(on_device, mesh.shape["sec"], mesh.shape["depth"]),
        mesh=mesh, in_specs=in_specs, out_specs=P("segment", None, "sec", "depth", None), check_vma=False,
    )
```
